256 devices in a mesh: brick: 128 (over x, z, y), state: 2 (over core).
Axes of the slice: x: 4, y: 4, z: 8, core: 2. Of those that a mesh axis runs over, the one named last changes fastest.
Arguments:
- states: bfloat16 [384, 884736], P('state', 'brick'), may hold values from -40 to 40
- kinetic: bfloat16 [343, 343], replicated, may hold values from -2 to 4, as said below
- potential: float32 [884736], P('brick'), may hold values from -1.5 to 1.5
- cell_nodes: int32 [4096, 343], P('brick'), may hold values from 0 to 8063, as said below
- face_map: int32 [147456], P('brick'), may hold values from 0 to 6911, as said below
Outputs:
- rotated: float32 [384, 884736], P('state', 'brick')
The draws below stay inside these ranges and needn't reach their ends.
Inputs may be any that keep to these rules, and one draw needn't show every extreme that they name: `cell_nodes`: block b of 32 rows belongs to brick b; a row lists the 343 nodes of one hexahedral cell of degree 6, lexicographic in the cell's three local coordinates, the first slowest. A value below 6912 is a column of brick b's block of states and potential; a value 6912 + f is the node named by entry f of brick b + 1's block of face_map (brick 0 after the last). Every own node and every face slot lies in some cell. `face_map`: block b of 1152 entries lists distinct own nodes of brick b: those it shares with brick b - 1. `kinetic`: Symmetric.
All inputs are finite; a program needn't handle non-finite values.
Results may differ from the reference program's by a relative error of at most 0.0005.
The reference program's roundings to bfloat16 on the way (of `filtered_once`, `filtered` and `root_rounded`) count: a program that leaves them out, or rounds other values in their place, can miss the bound.
Values may be sent and summed in bfloat16 or wider, within the bound.
A program may use at most 128 MiB of HBM per device.

```python
import math
import jax
import jax.numpy as jnp
from jax import lax

DEG = 6
STATES = 384
CX = 1
CY = 4
CZ = 8
NS_STEPS = 3
CELLS = 32
OWN = 6912
FACE = 1152
NODES = 884736
CELLS_ALL = 4096
FACES_ALL = 147456
N_BRICK = 128


def brick_numbering(key, brick_id):
    brick_seed = jax.random.fold_in(jax.random.fold_in(key, 7311), brick_id)
    numbering = jax.random.permutation(brick_seed, OWN).astype(jnp.int32)
    top_at = jnp.argmax(numbering == OWN - 1)
    numbering = numbering.at[top_at].set(numbering[0]).at[0].set(OWN - 1)
    low_at = jnp.argmax(numbering == 0)
    numbering = numbering.at[low_at].set(numbering[1]).at[1].set(0)
    return numbering


def brick_cells(key, brick_id):
    numbering = brick_numbering(key, brick_id)
    side_x = DEG * CX
    side_y = DEG * CY
    side_z = DEG * CZ
    cell_seed = jax.random.fold_in(jax.random.fold_in(key, 9157), brick_id)
    cell_order = jax.random.permutation(cell_seed, CELLS).astype(jnp.int32)
    cell_x = cell_order // (CY * CZ)
    cell_y = cell_order // CZ % CY
    cell_z = cell_order % CZ
    local_node = jnp.arange((DEG + 1) ** 3, dtype=jnp.int32)
    along_x = local_node // (DEG + 1) ** 2
    along_y = local_node // (DEG + 1) % (DEG + 1)
    along_z = local_node % (DEG + 1)
    plane_x = DEG * cell_x[:, None] + along_x[None, :]
    row_y = (DEG * cell_y[:, None] + along_y[None, :]) % side_y
    row_z = (DEG * cell_z[:, None] + along_z[None, :]) % side_z
    canonical = (jnp.minimum(plane_x, side_x - 1) * side_y + row_y) * side_z + row_z
    return jnp.where(plane_x < side_x, numbering[canonical], OWN + row_y * side_z + row_z).astype(jnp.int32)


def draw_cell_nodes(key, part):
    bricks = CELLS_ALL // CELLS
    blocks = jax.vmap(lambda brick_id: brick_cells(key, brick_id))(jnp.arange(bricks, dtype=jnp.int32))
    return blocks.reshape(CELLS_ALL, (DEG + 1) ** 3)


def draw_face_map(key, part):
    bricks = CELLS_ALL // CELLS
    blocks = jax.vmap(lambda brick_id: brick_numbering(key, brick_id)[:FACE])(jnp.arange(bricks, dtype=jnp.int32))
    return blocks.reshape(FACES_ALL)


def draw_states(key, part):
    bricks = CELLS_ALL // CELLS
    base_key = jax.random.fold_in(key, 0)
    column_key = jax.random.fold_in(key, 1)
    mixing_key = jax.random.fold_in(key, 4)
    brick_of_node = (jnp.arange(NODES) // OWN).astype(jnp.float32)
    node_scale = 1.0 + 2.0 * brick_of_node / max(bricks - 1, 1)
    state_scale = jnp.exp(jax.random.uniform(column_key, (STATES,), minval=math.log(0.3), maxval=math.log(3.0)))
    values = jnp.clip(jax.random.normal(base_key, (STATES, NODES)), -4.0, 4.0)
    blocks = values.reshape(STATES, bricks, OWN).transpose(1, 0, 2)

    def mix_one(inputs):
        brick_id, block = inputs
        noise = jnp.clip(jax.random.normal(jax.random.fold_in(mixing_key, brick_id), (STATES, STATES)), -4.0, 4.0)
        mixing = jnp.eye(STATES, dtype=jnp.float32) + 0.7 * noise / math.sqrt(STATES)
        return jnp.dot(mixing, block, precision=lax.Precision.HIGHEST)
    mixed_blocks = lax.map(mix_one, (jnp.arange(bricks, dtype=jnp.int32), blocks))
    mixed = mixed_blocks.transpose(1, 0, 2).reshape(STATES, NODES)
    result = mixed * state_scale[:, None] * node_scale[None, :]
    return jnp.clip(result, -40.0, 40.0).astype(jnp.bfloat16)


def draw_kinetic(key, part):
    width = (DEG + 1) ** 3
    first_key, second_key = jax.random.split(key, 2)
    noise = jnp.clip(jax.random.normal(first_key, (width, width)), -4.0, 4.0)
    symmetric = 0.5 * (noise + noise.T) / math.sqrt(width)
    diagonal = jnp.exp(jax.random.uniform(second_key, (width,), minval=math.log(0.3), maxval=math.log(1.5)))
    return (symmetric + jnp.diag(diagonal)).astype(jnp.bfloat16)


def block_levels(stream_key, shape, cuts, least, largest):
    gain = 1.0
    for dim, shards_of in cuts:
        heights = jax.random.uniform(jax.random.fold_in(jax.random.fold_in(stream_key, 6), dim), (shards_of,), jnp.float32, least / len(cuts), largest / len(cuts))
        gain = gain * jnp.repeat(jnp.exp(heights), shape[dim] // shards_of).reshape((-1,) + (1,) * (len(shape) - 1 - dim))
    return gain


def setup_inputs(seed: int = 0) -> dict:
    arg_keys = jax.random.split(jax.random.key(seed), 6)
    return {
        "states": draw_states(jax.random.fold_in(arg_keys[5], 71), 0),
        "kinetic": draw_kinetic(jax.random.fold_in(arg_keys[5], 71), 0),
        "potential": jnp.clip(jax.random.uniform(arg_keys[2], (NODES,), jnp.float32, -1.5, 1.5) * block_levels(arg_keys[2], (NODES,), ((0, 128),), -0.4, 0.0), -1.5, 1.5),
        "cell_nodes": draw_cell_nodes(jax.random.fold_in(arg_keys[5], 71), 0),
        "face_map": draw_face_map(jax.random.fold_in(arg_keys[5], 71), 0),
    }


cheb_center = 3.0
cheb_half = 7.0
epsilon = 1e-06

def global_numbering(cell_nodes, face_map):
    brick_of_cell = (jnp.arange(CELLS_ALL, dtype=jnp.int32) // CELLS)[:, None]
    next_brick = (brick_of_cell + 1) % N_BRICK
    is_ghost = cell_nodes >= OWN
    face_slot = jnp.clip(cell_nodes - OWN, 0, FACE - 1).astype(jnp.int32)
    ghost_target = face_map[(next_brick * FACE + face_slot).astype(jnp.int32)]
    return jnp.where(is_ghost, next_brick * OWN + ghost_target, brick_of_cell * OWN + cell_nodes).astype(jnp.int32)

def apply_operator(vector, kinetic, potential, global_nodes):
    total_nodes, width = vector.shape
    block_width = math.gcd(width, 64)
    kinetic_wide = kinetic.astype(jnp.float32)
    index_table = global_nodes.T
    flat_index = index_table.reshape(-1)
    per_cell = kinetic.shape[0]

    def one_block(column_block):
        gathered = column_block[index_table].astype(jnp.float32).reshape(per_cell, -1)
        products = jnp.dot(kinetic_wide, gathered, precision=lax.Precision.HIGHEST, preferred_element_type=jnp.float32)
        return jax.ops.segment_sum(products.reshape(-1, block_width), flat_index, num_segments=total_nodes)
    pieces = vector.reshape(total_nodes, width // block_width, block_width).transpose(1, 0, 2)
    result = lax.map(one_block, pieces).transpose(1, 0, 2).reshape(total_nodes, width)
    return result + potential[:, None] * vector.astype(jnp.float32)

def newton_schulz(margin):
    total = margin.shape[0]
    identity = jnp.eye(total, dtype=margin.dtype)
    scale = jnp.sqrt(jnp.sum(margin * margin) + epsilon)
    current = margin / scale
    inverse = identity
    for iteration in range(NS_STEPS):
        factor = 3.0 * identity - jnp.dot(inverse, current, precision=lax.Precision.HIGHEST)
        current = 0.5 * jnp.dot(factor, current, precision=lax.Precision.HIGHEST)
        inverse = 0.5 * jnp.dot(factor, inverse, precision=lax.Precision.HIGHEST)
    return inverse

def reference(states, kinetic, potential, cell_nodes, face_map):
    node_major = states.T
    global_nodes = global_numbering(cell_nodes, face_map)
    first = apply_operator(node_major, kinetic, potential, global_nodes)
    filtered_once = ((first - cheb_center * node_major.astype(jnp.float32)) / cheb_half).astype(jnp.bfloat16)
    second = apply_operator(filtered_once, kinetic, potential, global_nodes)
    filtered = (2.0 * (second - cheb_center * filtered_once.astype(jnp.float32)) / cheb_half - node_major.astype(jnp.float32)).astype(jnp.bfloat16)
    wide = filtered.astype(jnp.float32)
    margin = lax.dot_general(wide, wide, (((0,), (0,)), ((), ())), precision=lax.Precision.HIGHEST, preferred_element_type=jnp.float32)
    inverse_root = newton_schulz(margin)
    root_rounded = inverse_root.astype(jnp.bfloat16).astype(jnp.float32)
    return lax.dot_general(root_rounded, wide, (((1,), (1,)), ((), ())), precision=lax.Precision.HIGHEST, preferred_element_type=jnp.float32)
```

```python
import jax
import jax.numpy as jnp
from jax import lax
from jax.sharding import PartitionSpec as P

NS_STEPS = 3


cheb_center = 3.0
cheb_half = 7.0
epsilon = 1e-06


def passed_along(value, axis, steps):
    count = lax.axis_size(axis)
    pairs = [(source, (source + steps) % count) for source in range(count)]
    return lax.ppermute(value, axis, pairs)


def apply_operator(vector, kinetic, potential, cell_nodes, face_map):
    width, owned = vector.shape
    face_count = face_map.shape[0]
    ghost_cols = passed_along(vector[:, face_map], "brick", -1)
    extended = jnp.concatenate([vector, ghost_cols], axis=1)
    gathered = extended[:, cell_nodes]
    products = jnp.einsum("wca,ea->wce", gathered, kinetic, preferred_element_type=jnp.float32)
    summed = (
        jnp.zeros((width, owned + face_count), jnp.float32)
        .at[:, cell_nodes.reshape(-1)]
        .add(products.reshape(width, -1))
    )
    returned = passed_along(summed[:, owned:], "brick", 1)
    assembled = summed[:, :owned].at[:, face_map].add(returned)
    return assembled + potential[None, :] * vector.astype(jnp.float32)


def newton_schulz(margin):
    total = margin.shape[0]
    scale = jnp.sqrt(jnp.sum(margin * margin) + epsilon)
    current = margin / scale
    row_ids = lax.broadcasted_iota(jnp.int32, (total, total), 0)
    column_ids = lax.broadcasted_iota(jnp.int32, (total, total), 1)
    three = 3.0 * (row_ids == column_ids).astype(jnp.float32)
    factor = three - current
    current = 0.5 * jnp.dot(factor, current, precision=lax.Precision.HIGHEST)
    inverse = 0.5 * factor
    for iteration in range(1, NS_STEPS):
        factor = three - jnp.dot(inverse, current, precision=lax.Precision.HIGHEST)
        if iteration < NS_STEPS - 1:
            current = 0.5 * jnp.dot(factor, current, precision=lax.Precision.HIGHEST)
        inverse = 0.5 * jnp.dot(factor, inverse, precision=lax.Precision.HIGHEST)
    return inverse


def local(states, kinetic, potential, cell_nodes, face_map):
    first = apply_operator(states, kinetic, potential, cell_nodes, face_map)
    filtered_once = ((first - cheb_center * states.astype(jnp.float32)) / cheb_half).astype(
        jnp.bfloat16
    )
    second = apply_operator(filtered_once, kinetic, potential, cell_nodes, face_map)
    filtered = (
        2.0 * (second - cheb_center * filtered_once.astype(jnp.float32)) / cheb_half
        - states.astype(jnp.float32)
    ).astype(jnp.bfloat16)
    width = states.shape[0]
    every = lax.all_gather(filtered, "state", axis=0, tiled=True)
    side = lax.axis_index("state")
    half = every.shape[1] // 2
    share = lax.dynamic_slice_in_dim(every, side * half, half, axis=1)
    partial = lax.dot_general(
        share, share, (((1,), (1,)), ((), ())), preferred_element_type=jnp.float32
    )
    margin = lax.psum(partial, ("brick", "state"))
    root = newton_schulz(margin)
    root_rows = lax.dynamic_slice_in_dim(root, side * width, width, axis=0)
    return jnp.dot(root_rows.astype(jnp.bfloat16), every, preferred_element_type=jnp.float32)


def solution(mesh):
    in_specs = (P("state", "brick"), P(), P("brick"), P("brick", None), P("brick"))
    out_specs = P("state", "brick")
    return jax.shard_map(local, mesh=mesh, in_specs=in_specs, out_specs=out_specs, check_vma=False)
```

```python
import functools

import jax
import jax.numpy as jnp
from jax import lax
from jax.experimental import pallas as pl
from jax.experimental.pallas import tpu as pltpu
from jax.sharding import PartitionSpec as P

NS_STEPS = 3
LANES = 128
BATCH = 24

cheb_center = 3.0
cheb_half = 7.0
epsilon = 1e-06

VMEM = pltpu.VMEM
SMEM = pltpu.SMEM


def block(space):
    return pl.BlockSpec(memory_space=space)


def passed_along(value, axis, steps):
    count = lax.axis_size(axis)
    pairs = [(source, (source + steps) % count) for source in range(count)]
    return lax.ppermute(value, axis, pairs)


def even(start):
    return pl.ds(start, LANES, stride=2)


def tile_start(tile):
    return pl.multiple_of(tile * (2 * LANES), 2 * LANES)


def padded(value):
    return jnp.concatenate([value, jnp.zeros((value.shape[0], LANES - value.shape[1]), value.dtype)], axis=1)


def spread(compact, tile, width):
    rows = compact[pl.ds(pl.multiple_of(tile * LANES, LANES), LANES), :].astype(jnp.float32)
    return rows[:, :LANES], padded(rows[:, LANES:width])


def pair_row(ref, row):
    return ref[pl.ds(row, 2), :]


def gather_rows(source, target, index, base, count):
    for row in range(count):
        target[2 * row : 2 * row + 2, :] = pair_row(source, index[base + row])


def add_rows(total, addend, index, base, count):
    for first in range(0, count, BATCH):
        rows = range(first, min(first + BATCH, count))
        places = [index[base + row] for row in rows]
        sums = [pair_row(total, place) + addend[2 * row : 2 * row + 2, :] for place, row in zip(places, rows)]
        for place, value in zip(places, sums):
            total[pl.ds(place, 2), :] = value


def transpose_kernel(width, states, face, table, faces, held):
    tiles = states.shape[1] // LANES
    face_count = faces.shape[0]

    def one(tile, carry):
        nodes = pl.ds(pl.multiple_of(tile * LANES, LANES), LANES)
        low = states[:LANES, nodes].astype(jnp.float32)
        high = states[LANES:width, nodes].astype(jnp.float32)
        high = jnp.concatenate([high, jnp.zeros((2 * LANES - width, LANES), jnp.float32)], axis=0)
        start = tile_start(tile)
        table[even(start), :] = low.T
        table[even(start + 1), :] = high.T
        return carry

    lax.fori_loop(0, tiles, one, 0)

    def some_faces(tile, carry):
        gather_rows(table, held, face, tile * LANES, LANES)
        rows = pl.ds(pl.multiple_of(tile * LANES, LANES), LANES)
        faces[rows, :LANES] = held[even(0), :].astype(faces.dtype)
        faces[rows, LANES:width] = held[even(1), :][:, : width - LANES].astype(faces.dtype)
        return carry

    lax.fori_loop(0, face_count // LANES, some_faces, 0)


def start_sums(table, total, potential, owned, ghosts):
    def one(tile, carry):
        factor = jnp.broadcast_to(potential[pl.ds(tile, 1), :], (LANES, LANES)).T - cheb_center
        start = tile_start(tile)
        total[even(start), :] = factor * table[even(start), :]
        total[even(start + 1), :] = factor * table[even(start + 1), :]
        return carry

    lax.fori_loop(0, owned // LANES, one, 0)
    total[2 * owned :, :] = jnp.zeros((2 * ghosts, LANES), jnp.float32)


def apply_cells(table, total, kinetic, index, slots, held, product):
    depth = kinetic.shape[0]
    held[2 * slots :, :] = jnp.zeros((2 * (depth - slots), LANES), jnp.float32)

    def one(cell, carry):
        base = cell * slots
        gather_rows(table, held, index, base, slots)
        values = jnp.concatenate(
            [held[pl.ds(0, depth, stride=2), :], held[pl.ds(1, depth, stride=2), :]], axis=1
        ).astype(jnp.bfloat16)
        result = jnp.dot(kinetic[...], values, preferred_element_type=jnp.float32)
        product[pl.ds(0, depth, stride=2), :] = result[:, :LANES]
        product[pl.ds(1, depth, stride=2), :] = result[:, LANES:]
        add_rows(total, product, index, base, slots)
        return carry

    lax.fori_loop(0, index.shape[0] // slots, one, 0)


def give_ghosts(total, owned, out, width):
    def one(tile, carry):
        start = tile_start(tile) + 2 * owned
        rows = pl.ds(pl.multiple_of(tile * LANES, LANES), LANES)
        out[rows, :LANES] = total[even(start), :]
        out[rows, LANES:width] = total[even(start + 1), :][:, : width - LANES]
        return carry

    lax.fori_loop(0, out.shape[0] // LANES, one, 0)


def first_kernel(
    width, slots, states_table, ghosts, potential, kinetic, index, face, total, ghost_out, face_out,
    table, held, product, sem,
):
    owned = states_table.shape[0] // 2
    face_count = ghosts.shape[0]
    copy = pltpu.make_async_copy(states_table, table.at[pl.ds(0, 2 * owned), :], sem)
    copy.start()

    def fill(tile, carry):
        start = tile_start(tile) + 2 * owned
        low, high = spread(ghosts, tile, width)
        table[even(start), :] = low
        table[even(start + 1), :] = high
        return carry

    lax.fori_loop(0, face_count // LANES, fill, 0)
    copy.wait()
    start_sums(table, total, potential, owned, face_count)
    apply_cells(table, total, kinetic, index, slots, held, product)
    give_ghosts(total, owned, ghost_out, width)

    def some_faces(tile, carry):
        gather_rows(total, held, face, tile * LANES, LANES)
        rows = pl.ds(pl.multiple_of(tile * LANES, LANES), LANES)
        face_out[rows, :LANES] = held[even(0), :]
        face_out[rows, LANES:width] = held[even(1), :][:, : width - LANES]
        return carry

    lax.fori_loop(0, face_count // LANES, some_faces, 0)


def add_returned(total, returned, face, held, width):
    def one(tile, carry):
        low, high = spread(returned, tile, width)
        held[even(0), :] = low
        held[even(1), :] = high
        add_rows(total, held, face, tile * LANES, LANES)
        return carry

    lax.fori_loop(0, returned.shape[0] // LANES, one, 0)


def second_kernel(
    width, slots, first_total, returned, ghost_sums, potential, kinetic, index, face, total, ghost_out,
    table, held, product, sem,
):
    rows_all = first_total.shape[0]
    face_count = returned.shape[0]
    owned = rows_all // 2 - face_count
    copy = pltpu.make_async_copy(first_total, table, sem)
    copy.start()
    copy.wait()
    add_returned(table, returned, face, held, width)

    def fill(tile, carry):
        start = tile_start(tile) + 2 * owned
        low, high = spread(ghost_sums, tile, width)
        table[even(start), :] = table[even(start), :] + low
        table[even(start + 1), :] = table[even(start + 1), :] + high
        return carry

    lax.fori_loop(0, face_count // LANES, fill, 0)

    def scale(tile, carry):
        rows = pl.ds(tile_start(tile), 2 * LANES)
        table[rows, :] = (table[rows, :] / cheb_half).astype(jnp.bfloat16).astype(jnp.float32)
        return carry

    lax.fori_loop(0, rows_all // (2 * LANES), scale, 0)
    start_sums(table, total, potential, owned, face_count)
    apply_cells(table, total, kinetic, index, slots, held, product)
    give_ghosts(total, owned, ghost_out, width)


def last_kernel(width, total_in, states_table, returned, face, filtered, total, table, held, sems):
    owned = filtered.shape[0]
    copies = [
        pltpu.make_async_copy(total_in.at[pl.ds(0, 2 * owned), :], total, sems.at[0]),
        pltpu.make_async_copy(states_table, table, sems.at[1]),
    ]
    for copy in copies:
        copy.start()
    copies[0].wait()
    add_returned(total, returned, face, held, width)
    copies[1].wait()

    def one(tile, carry):
        start = tile_start(tile)
        rows = pl.ds(pl.multiple_of(tile * LANES, LANES), LANES)
        low = 2.0 * total[even(start), :] / cheb_half - table[even(start), :]
        high = 2.0 * total[even(start + 1), :] / cheb_half - table[even(start + 1), :]
        filtered[rows, :LANES] = low.astype(filtered.dtype)
        filtered[rows, LANES:width] = high[:, : width - LANES].astype(filtered.dtype)
        return carry

    lax.fori_loop(0, owned // LANES, one, 0)


def filter_states(states, kinetic, potential, cell_nodes, face_map):
    width, owned = states.shape
    cells, slots = cell_nodes.shape
    face_count = face_map.shape[0]
    depth = -(-slots // 16) * 16
    f32 = jnp.float32
    face = 2 * face_map
    index = 2 * cell_nodes.reshape(-1)
    potential = potential.reshape(-1, LANES)
    kinetic = jnp.pad(kinetic, ((0, depth - slots), (0, depth - slots)))
    rows_all = 2 * (owned + face_count)
    work = [VMEM((2 * depth, LANES), f32), VMEM((2 * depth, LANES), f32)]
    params = pltpu.CompilerParams(vmem_limit_bytes=40 << 20)

    table, faces = pl.pallas_call(
        functools.partial(transpose_kernel, width),
        name="transpose_states",
        out_shape=(
            jax.ShapeDtypeStruct((2 * owned, LANES), f32),
            jax.ShapeDtypeStruct((face_count, width), states.dtype),
        ),
        in_specs=[block(VMEM), block(SMEM)],
        out_specs=(block(VMEM), block(VMEM)),
        scratch_shapes=[VMEM((2 * LANES, LANES), f32)],
        compiler_params=params,
    )(states, face)
    ghosts = passed_along(faces, "brick", -1)
    compact = jax.ShapeDtypeStruct((face_count, width), f32)
    first, ghost_part, face_part = pl.pallas_call(
        functools.partial(first_kernel, width, slots),
        name="first_apply",
        out_shape=(jax.ShapeDtypeStruct((rows_all, LANES), f32), compact, compact),
        in_specs=[block(pl.ANY)] + [block(VMEM)] * 3 + [block(SMEM)] * 2,
        out_specs=(block(VMEM),) * 3,
        scratch_shapes=[VMEM((rows_all, LANES), f32)] + work + [pltpu.SemaphoreType.DMA],
        compiler_params=params,
    )(table, ghosts, potential, kinetic, index, face)
    returned = passed_along(ghost_part, "brick", 1)
    ghost_sums = passed_along(face_part, "brick", -1)
    second, ghost_part = pl.pallas_call(
        functools.partial(second_kernel, width, slots),
        name="second_apply",
        out_shape=(jax.ShapeDtypeStruct((rows_all, LANES), f32), compact),
        in_specs=[block(pl.ANY)] + [block(VMEM)] * 4 + [block(SMEM)] * 2,
        out_specs=(block(VMEM),) * 2,
        scratch_shapes=[VMEM((rows_all, LANES), f32)] + work + [pltpu.SemaphoreType.DMA],
        compiler_params=params,
    )(first, returned, ghost_sums, potential, kinetic, index, face)
    returned = passed_along(ghost_part, "brick", 1)
    return pl.pallas_call(
        functools.partial(last_kernel, width),
        name="finish_filter",
        out_shape=jax.ShapeDtypeStruct((owned, width), jnp.bfloat16),
        in_specs=[block(pl.ANY)] * 2 + [block(VMEM), block(SMEM)],
        out_specs=block(VMEM),
        scratch_shapes=[VMEM((2 * owned, LANES), f32)] * 2
        + [VMEM((2 * LANES, LANES), f32), pltpu.SemaphoreType.DMA((2,))],
        compiler_params=params,
    )(second, table, returned, face)


def newton_schulz(margin):
    total = margin.shape[0]
    scale = jnp.sqrt(jnp.sum(margin * margin) + epsilon)
    current = margin / scale
    row_ids = lax.broadcasted_iota(jnp.int32, (total, total), 0)
    column_ids = lax.broadcasted_iota(jnp.int32, (total, total), 1)
    three = 3.0 * (row_ids == column_ids).astype(jnp.float32)
    factor = three - current
    current = 0.5 * jnp.dot(factor, current, precision=lax.Precision.HIGHEST)
    inverse = 0.5 * factor
    for iteration in range(1, NS_STEPS):
        factor = three - jnp.dot(inverse, current, precision=lax.Precision.HIGHEST)
        if iteration < NS_STEPS - 1:
            current = 0.5 * jnp.dot(factor, current, precision=lax.Precision.HIGHEST)
        inverse = 0.5 * jnp.dot(factor, inverse, precision=lax.Precision.HIGHEST)
    return inverse


def local(states, kinetic, potential, cell_nodes, face_map):
    filtered = filter_states(states, kinetic, potential, cell_nodes, face_map)
    owned, width = filtered.shape
    every = lax.all_gather(filtered, "state", axis=1, tiled=True)
    side = lax.axis_index("state")
    half = owned // 2
    share = lax.dynamic_slice_in_dim(every, side * half, half, axis=0)
    partial = lax.dot_general(
        share, share, (((0,), (0,)), ((), ())), preferred_element_type=jnp.float32
    )
    margin = lax.psum(partial, ("brick", "state"))
    root = newton_schulz(margin)
    root_rows = lax.dynamic_slice_in_dim(root, side * width, width, axis=0)
    return lax.dot_general(
        root_rows.astype(jnp.bfloat16), every, (((1,), (1,)), ((), ())),
        preferred_element_type=jnp.float32,
    )


def solution(mesh):
    in_specs = (P("state", "brick"), P(), P("brick"), P("brick", None), P("brick"))
    out_specs = P("state", "brick")
    return jax.shard_map(local, mesh=mesh, in_specs=in_specs, out_specs=out_specs, check_vma=False)
```

```python
import functools

import jax
import jax.numpy as jnp
from jax import lax
from jax.experimental import pallas as pl
from jax.experimental.pallas import tpu as pltpu
from jax.sharding import PartitionSpec as P

NS_STEPS = 3
LANES = 128
BATCH = 24

cheb_center = 3.0
cheb_half = 7.0
epsilon = 1e-06

VMEM = pltpu.VMEM
SMEM = pltpu.SMEM


def block(space):
    return pl.BlockSpec(memory_space=space)


def passed_along(value, axis, steps):
    count = lax.axis_size(axis)
    pairs = [(source, (source + steps) % count) for source in range(count)]
    return lax.ppermute(value, axis, pairs)


def even(start):
    return pl.ds(start, LANES, stride=2)


def tile_start(tile):
    return pl.multiple_of(tile * (2 * LANES), 2 * LANES)


def padded(value):
    return jnp.concatenate([value, jnp.zeros((value.shape[0], LANES - value.shape[1]), value.dtype)], axis=1)


def spread(compact, tile, width):
    rows = compact[pl.ds(pl.multiple_of(tile * LANES, LANES), LANES), :].astype(jnp.float32)
    return rows[:, :LANES], padded(rows[:, LANES:width])


def pair_row(ref, row):
    return ref[pl.ds(row, 2), :]


def gather_rows(source, target, index, base, count):
    for row in range(count):
        target[2 * row : 2 * row + 2, :] = pair_row(source, index[base + row])


def add_rows(total, addend, index, base, count):
    for first in range(0, count, BATCH):
        rows = range(first, min(first + BATCH, count))
        places = [index[base + row] for row in rows]
        sums = [pair_row(total, place) + addend[2 * row : 2 * row + 2, :] for place, row in zip(places, rows)]
        for place, value in zip(places, sums):
            total[pl.ds(place, 2), :] = value


def transpose_kernel(width, states, face, table, faces, held):
    tiles = states.shape[1] // LANES
    face_count = faces.shape[0]

    def one(tile, carry):
        nodes = pl.ds(pl.multiple_of(tile * LANES, LANES), LANES)
        low = states[:LANES, nodes].astype(jnp.float32)
        high = states[LANES:width, nodes].astype(jnp.float32)
        high = jnp.concatenate([high, jnp.zeros((2 * LANES - width, LANES), jnp.float32)], axis=0)
        start = tile_start(tile)
        table[even(start), :] = low.T
        table[even(start + 1), :] = high.T
        return carry

    lax.fori_loop(0, tiles, one, 0)

    def some_faces(tile, carry):
        gather_rows(table, held, face, tile * LANES, LANES)
        rows = pl.ds(pl.multiple_of(tile * LANES, LANES), LANES)
        faces[rows, :LANES] = held[even(0), :].astype(faces.dtype)
        faces[rows, LANES:width] = held[even(1), :][:, : width - LANES].astype(faces.dtype)
        return carry

    lax.fori_loop(0, face_count // LANES, some_faces, 0)


def start_sums(table, total, potential, owned, ghosts):
    def one(tile, carry):
        factor = jnp.broadcast_to(potential[pl.ds(tile, 1), :], (LANES, LANES)).T - cheb_center
        start = tile_start(tile)
        total[even(start), :] = factor * table[even(start), :]
        total[even(start + 1), :] = factor * table[even(start + 1), :]
        return carry

    lax.fori_loop(0, owned // LANES, one, 0)
    total[2 * owned :, :] = jnp.zeros((2 * ghosts, LANES), jnp.float32)


def apply_cells(table, total, kinetic, index, slots, held, product):
    depth = kinetic.shape[0]
    held[2 * slots :, :] = jnp.zeros((2 * (depth - slots), LANES), jnp.float32)

    def one(cell, carry):
        base = cell * slots
        gather_rows(table, held, index, base, slots)
        values = jnp.concatenate(
            [held[pl.ds(0, depth, stride=2), :], held[pl.ds(1, depth, stride=2), :]], axis=1
        ).astype(jnp.bfloat16)
        result = jnp.dot(kinetic[...], values, preferred_element_type=jnp.float32)
        product[pl.ds(0, depth, stride=2), :] = result[:, :LANES]
        product[pl.ds(1, depth, stride=2), :] = result[:, LANES:]
        add_rows(total, product, index, base, slots)
        return carry

    lax.fori_loop(0, index.shape[0] // slots, one, 0)


def give_ghosts(total, owned, out, width):
    def one(tile, carry):
        start = tile_start(tile) + 2 * owned
        rows = pl.ds(pl.multiple_of(tile * LANES, LANES), LANES)
        out[rows, :LANES] = total[even(start), :]
        out[rows, LANES:width] = total[even(start + 1), :][:, : width - LANES]
        return carry

    lax.fori_loop(0, out.shape[0] // LANES, one, 0)


def first_kernel(
    width, slots, states_table, ghosts, potential, kinetic, index, face, total, ghost_out, face_out,
    table, held, product, sem,
):
    owned = states_table.shape[0] // 2
    face_count = ghosts.shape[0]
    copy = pltpu.make_async_copy(states_table, table.at[pl.ds(0, 2 * owned), :], sem)
    copy.start()

    def fill(tile, carry):
        start = tile_start(tile) + 2 * owned
        low, high = spread(ghosts, tile, width)
        table[even(start), :] = low
        table[even(start + 1), :] = high
        return carry

    lax.fori_loop(0, face_count // LANES, fill, 0)
    copy.wait()
    start_sums(table, total, potential, owned, face_count)
    apply_cells(table, total, kinetic, index, slots, held, product)
    give_ghosts(total, owned, ghost_out, width)

    def some_faces(tile, carry):
        gather_rows(total, held, face, tile * LANES, LANES)
        rows = pl.ds(pl.multiple_of(tile * LANES, LANES), LANES)
        face_out[rows, :LANES] = held[even(0), :]
        face_out[rows, LANES:width] = held[even(1), :][:, : width - LANES]
        return carry

    lax.fori_loop(0, face_count // LANES, some_faces, 0)


def add_returned(total, returned, face, held, width):
    def one(tile, carry):
        low, high = spread(returned, tile, width)
        held[even(0), :] = low
        held[even(1), :] = high
        add_rows(total, held, face, tile * LANES, LANES)
        return carry

    lax.fori_loop(0, returned.shape[0] // LANES, one, 0)


def second_kernel(
    width, slots, first_total, returned, ghost_sums, potential, kinetic, index, face, total, ghost_out,
    table, held, product, sem,
):
    rows_all = first_total.shape[0]
    face_count = returned.shape[0]
    owned = rows_all // 2 - face_count
    copy = pltpu.make_async_copy(first_total, table, sem)
    copy.start()
    copy.wait()
    add_returned(table, returned, face, held, width)

    def fill(tile, carry):
        start = tile_start(tile) + 2 * owned
        low, high = spread(ghost_sums, tile, width)
        table[even(start), :] = table[even(start), :] + low
        table[even(start + 1), :] = table[even(start + 1), :] + high
        return carry

    lax.fori_loop(0, face_count // LANES, fill, 0)

    def scale(tile, carry):
        rows = pl.ds(tile_start(tile), 2 * LANES)
        table[rows, :] = (table[rows, :] / cheb_half).astype(jnp.bfloat16).astype(jnp.float32)
        return carry

    lax.fori_loop(0, rows_all // (2 * LANES), scale, 0)
    start_sums(table, total, potential, owned, face_count)
    apply_cells(table, total, kinetic, index, slots, held, product)
    give_ghosts(total, owned, ghost_out, width)


def last_kernel(width, total_in, states_table, returned, face, filtered, total, table, held, sems):
    owned = filtered.shape[1]
    copies = [
        pltpu.make_async_copy(total_in.at[pl.ds(0, 2 * owned), :], total, sems.at[0]),
        pltpu.make_async_copy(states_table, table, sems.at[1]),
    ]
    for copy in copies:
        copy.start()
    copies[0].wait()
    add_returned(total, returned, face, held, width)
    copies[1].wait()

    def one(tile, carry):
        start = tile_start(tile)
        nodes = pl.ds(pl.multiple_of(tile * LANES, LANES), LANES)
        low = 2.0 * total[even(start), :] / cheb_half - table[even(start), :]
        high = 2.0 * total[even(start + 1), :] / cheb_half - table[even(start + 1), :]
        filtered[:LANES, nodes] = low.T.astype(filtered.dtype)
        filtered[LANES:width, nodes] = high.T[: width - LANES, :].astype(filtered.dtype)
        return carry

    lax.fori_loop(0, owned // LANES, one, 0)


def filter_states(states, kinetic, potential, cell_nodes, face_map):
    width, owned = states.shape
    cells, slots = cell_nodes.shape
    face_count = face_map.shape[0]
    depth = -(-slots // 16) * 16
    f32 = jnp.float32
    face = 2 * face_map
    index = 2 * cell_nodes.reshape(-1)
    potential = potential.reshape(-1, LANES)
    kinetic = jnp.pad(kinetic, ((0, depth - slots), (0, depth - slots)))
    rows_all = 2 * (owned + face_count)
    work = [VMEM((2 * depth, LANES), f32), VMEM((2 * depth, LANES), f32)]
    params = pltpu.CompilerParams(vmem_limit_bytes=40 << 20)

    table, faces = pl.pallas_call(
        functools.partial(transpose_kernel, width),
        name="transpose_states",
        out_shape=(
            jax.ShapeDtypeStruct((2 * owned, LANES), f32),
            jax.ShapeDtypeStruct((face_count, width), states.dtype),
        ),
        in_specs=[block(VMEM), block(SMEM)],
        out_specs=(block(VMEM), block(VMEM)),
        scratch_shapes=[VMEM((2 * LANES, LANES), f32)],
        compiler_params=params,
    )(states, face)
    ghosts = passed_along(faces, "brick", -1)
    compact = jax.ShapeDtypeStruct((face_count, width), f32)
    first, ghost_part, face_part = pl.pallas_call(
        functools.partial(first_kernel, width, slots),
        name="first_apply",
        out_shape=(jax.ShapeDtypeStruct((rows_all, LANES), f32), compact, compact),
        in_specs=[block(pl.ANY)] + [block(VMEM)] * 3 + [block(SMEM)] * 2,
        out_specs=(block(VMEM),) * 3,
        scratch_shapes=[VMEM((rows_all, LANES), f32)] + work + [pltpu.SemaphoreType.DMA],
        compiler_params=params,
    )(table, ghosts, potential, kinetic, index, face)
    returned = passed_along(ghost_part, "brick", 1)
    ghost_sums = passed_along(face_part, "brick", -1)
    second, ghost_part = pl.pallas_call(
        functools.partial(second_kernel, width, slots),
        name="second_apply",
        out_shape=(jax.ShapeDtypeStruct((rows_all, LANES), f32), compact),
        in_specs=[block(pl.ANY)] + [block(VMEM)] * 4 + [block(SMEM)] * 2,
        out_specs=(block(VMEM),) * 2,
        scratch_shapes=[VMEM((rows_all, LANES), f32)] + work + [pltpu.SemaphoreType.DMA],
        compiler_params=params,
    )(first, returned, ghost_sums, potential, kinetic, index, face)
    returned = passed_along(ghost_part, "brick", 1)
    return pl.pallas_call(
        functools.partial(last_kernel, width),
        name="finish_filter",
        out_shape=jax.ShapeDtypeStruct((width, owned), jnp.bfloat16),
        in_specs=[block(pl.ANY)] * 2 + [block(VMEM), block(SMEM)],
        out_specs=block(VMEM),
        scratch_shapes=[VMEM((2 * owned, LANES), f32)] * 2
        + [VMEM((2 * LANES, LANES), f32), pltpu.SemaphoreType.DMA((2,))],
        compiler_params=params,
    )(second, table, returned, face)


X_SIZE, Y_SIZE, Z_SIZE = 4, 4, 8
PLANE = X_SIZE * Y_SIZE
MESH = pl.DeviceIdType.MESH
EXACT = lax.Precision.HIGHEST
CHUNK = 768


def across(left, right):
    return lax.dot_general(left, right, (((1,), (1,)), ((), ())), preferred_element_type=jnp.float32)


def product_of(left, right):
    return jnp.dot(left, right, precision=EXACT, preferred_element_type=jnp.float32)


def unpack(packed):
    corner = packed[128:192, :]
    right = jnp.concatenate([corner.T, packed[288:352, 64:128]], axis=0)
    square = jnp.concatenate([packed[:192, :], right], axis=1)
    mixed = jnp.concatenate([packed[192:288, :], packed[288:384, :64]], axis=1)
    return square, mixed


def root_kernel(
    own, other, root_own, root_other,
    share, inbox, part, levels, own_all, other_all, square, mixed, current, inverse,
    state_sems, send_sems, plane_sems, level_sems, gather_sems, pair_sems,
):
    brick, side = lax.axis_index("brick"), lax.axis_index("state")
    width, owned = own.shape
    half = width // 2
    y, z, x = brick % Y_SIZE, (brick // Y_SIZE) % Z_SIZE, brick // (Y_SIZE * Z_SIZE)
    place = x * Y_SIZE + y

    def in_plane(step):
        target = (place + step) % PLANE
        return target, ((target // Y_SIZE) * Z_SIZE + z) * Y_SIZE + target % Y_SIZE

    def in_line(step):
        return (x * Z_SIZE + (z + step) % Z_SIZE) * Y_SIZE + y

    barrier = pltpu.get_barrier_semaphore()
    pl.semaphore_signal(barrier, inc=1, device_id=(brick, 1 - side), device_id_type=MESH)
    for step in range(1, PLANE):
        pl.semaphore_signal(barrier, inc=1, device_id=(in_plane(step)[1], side), device_id_type=MESH)
    for step in range(1, Z_SIZE):
        pl.semaphore_signal(barrier, inc=1, device_id=(in_line(step), side), device_id_type=MESH)
    pl.semaphore_wait(barrier, PLANE + Z_SIZE - 1)

    pieces = 3
    piece = owned // pieces
    states = []
    for number in range(pieces):
        columns = pl.ds(number * piece, piece)
        copy = pltpu.make_async_remote_copy(
            src_ref=own.at[:, columns], dst_ref=other.at[:, columns],
            send_sem=state_sems.at[0, number], recv_sem=state_sems.at[1, number],
            device_id=(brick, 1 - side), device_id_type=MESH,
        )
        copy.start()
        states.append(copy)

    square[...] = jnp.zeros_like(square)
    mixed[...] = jnp.zeros_like(mixed)

    def add_square(number, carry):
        values = own[:, pl.ds(pl.multiple_of(number * CHUNK, CHUNK), CHUNK)]
        square[...] += across(values, values)
        return carry

    lax.fori_loop(0, owned // CHUNK, add_square, 0)
    for number, copy in enumerate(states):
        copy.wait()

        def add_mixed(step, carry):
            columns = pl.ds(pl.multiple_of(number * piece + step * CHUNK, CHUNK), CHUNK)

            @pl.when(side == 0)
            def _():
                mixed[...] += across(own[:half, columns], other[:, columns])

            @pl.when(side == 1)
            def _():
                mixed[...] += across(other[half:, columns], own[:, columns])

            return carry

        lax.fori_loop(0, piece // CHUNK, add_mixed, 0)

    share[:192, :] = square[:, :128]
    share[192:288, :] = mixed[:, :128]
    share[288:352, :] = jnp.concatenate([mixed[:64, 128:], square[128:, 128:]], axis=1)
    share[352:384, :] = jnp.concatenate([mixed[64:, 128:], jnp.zeros((32, 64), jnp.float32)], axis=1)

    rows = share.shape[0] // PLANE
    copies = []
    for step in range(1, PLANE):
        target, chip = in_plane(step)
        copy = pltpu.make_async_remote_copy(
            src_ref=share.at[pl.ds(pl.multiple_of(target * rows, 8), rows), :], dst_ref=inbox.at[step - 1],
            send_sem=send_sems.at[step - 1], recv_sem=plane_sems.at[step - 1],
            device_id=(chip, side), device_id_type=MESH,
        )
        copy.start()
        copies.append(copy)
    value = share[pl.ds(pl.multiple_of(place * rows, 8), rows), :]
    for copy in copies:
        copy.wait()
    for step in range(PLANE - 1):
        value = value + inbox[step]
    part[...] = value
    levels[z] = value
    copies = []
    for step in range(1, Z_SIZE):
        copy = pltpu.make_async_remote_copy(
            src_ref=part, dst_ref=levels.at[z],
            send_sem=send_sems.at[PLANE - 2 + step], recv_sem=level_sems.at[step - 1],
            device_id=(in_line(step), side), device_id_type=MESH,
        )
        copy.start()
        copies.append(copy)
    for copy in copies:
        copy.wait()
    value = levels[0]
    for step in range(1, Z_SIZE):
        value = value + levels[step]
    own_all[place] = value
    copies = []
    for step in range(1, PLANE):
        copy = pltpu.make_async_remote_copy(
            src_ref=own_all.at[place], dst_ref=own_all.at[place],
            send_sem=send_sems.at[PLANE + Z_SIZE - 3 + step], recv_sem=gather_sems.at[step - 1],
            device_id=(in_plane(step)[1], side), device_id_type=MESH,
        )
        copy.start()
        copies.append(copy)
    for copy in copies:
        copy.wait()
    swap = pltpu.make_async_remote_copy(
        src_ref=own_all, dst_ref=other_all, send_sem=pair_sems.at[0], recv_sem=pair_sems.at[1],
        device_id=(brick, 1 - side), device_id_type=MESH,
    )
    swap.start()
    swap.wait()

    mine = own_all[...].reshape(PLANE * rows, 128)
    theirs = other_all[...].reshape(PLANE * rows, 128)
    first, first_mixed = unpack(jnp.where(side == 0, mine, theirs))
    second, second_mixed = unpack(jnp.where(side == 0, theirs, mine))
    both = jnp.concatenate([first_mixed, second_mixed], axis=0)
    margin = jnp.concatenate(
        [jnp.concatenate([first, both], axis=1), jnp.concatenate([both.T, second], axis=1)], axis=0
    )
    scale = jnp.sqrt(jnp.sum(margin * margin, axis=(0, 1), keepdims=True) + epsilon)
    total = margin.shape[0]
    row_ids = lax.broadcasted_iota(jnp.int32, (total, total), 0)
    column_ids = lax.broadcasted_iota(jnp.int32, (total, total), 1)
    three = jnp.where(row_ids == column_ids, 3.0, 0.0)
    start = margin / scale
    factor = three - start
    current[...] = 0.5 * product_of(factor, start)
    inverse[...] = 0.5 * factor
    for step in range(1, NS_STEPS - 1):
        factor = three - product_of(inverse[...], current[...])
        current[...] = 0.5 * product_of(factor, current[...])
        inverse[...] = 0.5 * product_of(factor, inverse[...])
    mine = pl.ds(pl.multiple_of(side * width, 8), width)
    row_ids = lax.broadcasted_iota(jnp.int32, (width, total), 0) + side * width
    column_ids = lax.broadcasted_iota(jnp.int32, (width, total), 1)
    factor = jnp.where(row_ids == column_ids, 3.0, 0.0) - product_of(inverse[mine, :], current[...])
    root = (0.5 * product_of(factor, inverse[...])).astype(root_own.dtype)
    left, right = root[:, :width], root[:, width:]
    root_own[...] = jnp.where(side == 0, left, right)
    root_other[...] = jnp.where(side == 0, right, left)


def inverse_root(filtered):
    width, owned = filtered.shape
    f32 = jnp.float32
    rows = 384 // PLANE
    square = jax.ShapeDtypeStruct((width, width), jnp.bfloat16)
    dma = pltpu.SemaphoreType.DMA
    return pl.pallas_call(
        root_kernel,
        name="inverse_root",
        out_shape=(jax.ShapeDtypeStruct((width, owned), filtered.dtype), square, square),
        in_specs=[block(VMEM)],
        out_specs=(block(VMEM),) * 3,
        scratch_shapes=[
            VMEM((384, 128), f32), VMEM((PLANE - 1, rows, 128), f32), VMEM((rows, 128), f32),
            VMEM((Z_SIZE, rows, 128), f32), VMEM((PLANE, rows, 128), f32), VMEM((PLANE, rows, 128), f32),
            VMEM((width, width), f32), VMEM((width // 2, width), f32),
            VMEM((2 * width, 2 * width), f32), VMEM((2 * width, 2 * width), f32),
            dma((2, 3)), dma((2 * PLANE + Z_SIZE - 3,)), dma((PLANE - 1,)), dma((Z_SIZE - 1,)),
            dma((PLANE - 1,)), dma((2,)),
        ],
        compiler_params=pltpu.CompilerParams(
            collective_id=0, has_side_effects=True, vmem_limit_bytes=32 << 20
        ),
    )(filtered)


def rotate_kernel(own, other, root_own, root_other, out):
    out[...] = jnp.dot(root_own[...], own[...], preferred_element_type=jnp.float32) + jnp.dot(
        root_other[...], other[...], preferred_element_type=jnp.float32
    )


def local(states, kinetic, potential, cell_nodes, face_map):
    filtered = filter_states(states, kinetic, potential, cell_nodes, face_map)
    width, owned = filtered.shape
    other, root_own, root_other = inverse_root(filtered)
    columns = pl.BlockSpec((width, CHUNK), lambda step: (0, step))
    whole = pl.BlockSpec((width, width), lambda step: (0, 0))
    return pl.pallas_call(
        rotate_kernel,
        name="rotate",
        grid=(owned // CHUNK,),
        out_shape=jax.ShapeDtypeStruct((width, owned), jnp.float32),
        in_specs=[columns, columns, whole, whole],
        out_specs=columns,
    )(filtered, other, root_own, root_other)


def solution(mesh):
    in_specs = (P("state", "brick"), P(), P("brick"), P("brick", None), P("brick"))
    out_specs = P("state", "brick")
    return jax.shard_map(local, mesh=mesh, in_specs=in_specs, out_specs=out_specs, check_vma=False)
```

```python
import functools

import jax
import jax.numpy as jnp
from jax import lax
from jax.experimental import pallas as pl
from jax.experimental.pallas import tpu as pltpu
from jax.sharding import PartitionSpec as P

NS_STEPS = 3
LANES = 128
BATCH = 24
GROUP = 4
LIMIT = 24 << 20

cheb_center = 3.0
cheb_half = 7.0
epsilon = 1e-06

VMEM = pltpu.VMEM
SMEM = pltpu.SMEM


def block(space):
    return pl.BlockSpec(memory_space=space)


def passed_along(value, axis, steps):
    count = lax.axis_size(axis)
    pairs = [(source, (source + steps) % count) for source in range(count)]
    return lax.ppermute(value, axis, pairs)


def even(start):
    return pl.ds(start, LANES, stride=2)


def tile_start(tile):
    return pl.multiple_of(tile * (2 * LANES), 2 * LANES)


def padded(value):
    return jnp.concatenate([value, jnp.zeros((value.shape[0], LANES - value.shape[1]), value.dtype)], axis=1)


def packed_rows(faces):
    return faces * 3 // 2


def pack(out, tile, low, high):
    faces = out.shape[0] * 2 // 3
    lane = lax.broadcasted_iota(jnp.int32, (LANES // 2, LANES), 1)
    joined = jnp.where(lane < LANES // 2, high[: LANES // 2], pltpu.roll(high[LANES // 2 :], LANES // 2, axis=1))
    out[tile * LANES : (tile + 1) * LANES, :] = low.astype(out.dtype)
    out[faces + tile * LANES // 2 : faces + (tile + 1) * LANES // 2, :] = joined.astype(out.dtype)


def unpack_rows(ref, tile):
    faces = ref.shape[0] * 2 // 3
    low = ref[tile * LANES : (tile + 1) * LANES, :].astype(jnp.float32)
    joined = ref[faces + tile * LANES // 2 : faces + (tile + 1) * LANES // 2, :].astype(jnp.float32)
    return low, jnp.concatenate([joined, pltpu.roll(joined, LANES // 2, axis=1)], axis=0)


def pair_row(ref, row):
    return ref[pl.ds(row, 2), :]


def gather_rows(source, target, places):
    for row, place in enumerate(places):
        target[2 * row : 2 * row + 2, :] = pair_row(source, place())


def add_rows(total, addend, places):
    for first in range(0, len(places), BATCH):
        rows = range(first, min(first + BATCH, len(places)))
        at = [places[row]() for row in rows]
        sums = [pair_row(total, place) + addend[2 * row : 2 * row + 2, :] for place, row in zip(at, rows)]
        for place, value in zip(at, sums):
            total[pl.ds(place, 2), :] = value


def entries(index, count, *lead):
    start = lead[-1] if lead else 0
    return [functools.partial(lambda i: index[i], start + row) for row in range(count)]


def gather_faces(source, held, face, out):
    for tile in range(face.shape[0] // LANES):
        buffer = held.at[tile % 2]
        gather_rows(source, buffer, entries(face, LANES, tile * LANES))
        pack(out, tile, buffer[even(0), :], buffer[even(1), :])


def fill_table(width, states, table):
    def one(tile, carry):
        nodes = pl.ds(pl.multiple_of(tile * LANES, LANES), LANES)
        low = states[:LANES, nodes].astype(jnp.float32)
        high = states[LANES:width, nodes].astype(jnp.float32)
        high = jnp.concatenate([high, jnp.zeros((2 * LANES - width, LANES), jnp.float32)], axis=0)
        start = tile_start(tile)
        table[even(start), :] = low.T
        table[even(start + 1), :] = high.T
        return carry

    lax.fori_loop(0, states.shape[1] // LANES, one, 0, unroll=2)


def copy_rows(source, target, count):
    def take(tile, carry):
        rows = pl.ds(tile_start(tile), 2 * LANES)
        target[rows, :] = source[rows, :]
        return carry

    lax.fori_loop(0, count // (2 * LANES), take, 0)


def faces_kernel(width, states, face, faces, table, held):
    fill_table(width, states, table)
    gather_faces(table, held, face, faces)


def start_sums(table, total, potential, owned, ghosts):
    def one(tile, carry):
        factor = jnp.broadcast_to(potential[pl.ds(tile, 1), :], (LANES, LANES)).T - cheb_center
        start = tile_start(tile)
        total[even(start), :] = factor * table[even(start), :]
        total[even(start + 1), :] = factor * table[even(start + 1), :]
        return carry

    lax.fori_loop(0, owned // LANES, one, 0)
    total[2 * owned :, :] = jnp.zeros((2 * ghosts, LANES), jnp.float32)


def apply_cells(table, total, kinetic, index, slots, held, product, places, sems):
    depth = kinetic.shape[0]
    groups, cells, _ = index.shape
    for side in range(2):
        held[side, 2 * slots :, :] = jnp.zeros((2 * (depth - slots), LANES), jnp.float32)

    def fetch(group, side):
        return pltpu.make_async_copy(index.at[group], places.at[side], sems.at[side])

    def one_group(group, side):
        fetch(group, side).wait()
        fetch(jnp.minimum(group + 1, groups - 1), 1 - side).start()
        for cell in range(cells):
            at = [functools.partial(lambda i: places[side, cell, i], row) for row in range(slots)]
            values, result = held.at[cell % 2], product.at[cell % 2]
            gather_rows(table, values, at)
            operand = jnp.concatenate(
                [values[pl.ds(0, depth, stride=2), :], values[pl.ds(1, depth, stride=2), :]], axis=1
            ).astype(jnp.bfloat16)
            answer = jnp.dot(kinetic[...], operand, preferred_element_type=jnp.float32)
            result[pl.ds(0, depth, stride=2), :] = answer[:, :LANES]
            result[pl.ds(1, depth, stride=2), :] = answer[:, LANES:]
            add_rows(total, result, at)

    fetch(0, 0).start()

    def two_groups(step, carry):
        one_group(2 * step, 0)
        one_group(2 * step + 1, 1)
        return carry

    lax.fori_loop(0, groups // 2, two_groups, 0)
    fetch(groups - 1, groups % 2).wait()


def give_ghosts(total, owned, out):
    for tile in range(out.shape[0] * 2 // 3 // LANES):
        start = 2 * owned + tile * 2 * LANES
        pack(out, tile, total[even(start), :], total[even(start + 1), :])


def first_kernel(
    width, slots, states, ghosts, potential, kinetic, index, face, sums, ghost_out, face_out,
    table, total, held, product, places, sems,
):
    owned = states.shape[1]
    face_count = face.shape[0]
    fill_table(width, states, table)
    for tile in range(face_count // LANES):
        start = 2 * owned + tile * 2 * LANES
        low, high = unpack_rows(ghosts, tile)
        table[even(start), :] = low
        table[even(start + 1), :] = high
    start_sums(table, total, potential, owned, face_count)
    apply_cells(table, total, kinetic, index, slots, held, product, places, sems)
    give_ghosts(total, owned, ghost_out)
    gather_faces(total, held, face, face_out)
    copy_rows(total, sums, total.shape[0])


def add_returned(total, returned, face, held):
    for tile in range(face.shape[0] // LANES):
        low, high = unpack_rows(returned, tile)
        buffer = held.at[tile % 2]
        buffer[even(0), :] = low
        buffer[even(1), :] = high
        add_rows(total, buffer, entries(face, LANES, tile * LANES))


def second_kernel(
    owned, slots, given, returned, ghost_sums, potential, kinetic, index, face, sums, ghost_out,
    table, total, held, product, places, sems,
):
    face_count = face.shape[0]
    rows_all = table.shape[0]
    copy_rows(given, table, rows_all)
    add_returned(table, returned, face, held)
    for tile in range(face_count // LANES):
        start = 2 * owned + tile * 2 * LANES
        low, high = unpack_rows(ghost_sums, tile)
        table[even(start), :] = table[even(start), :] + low
        table[even(start + 1), :] = table[even(start + 1), :] + high

    def scale(tile, carry):
        rows = pl.ds(tile_start(tile), 2 * LANES)
        table[rows, :] = (table[rows, :] / cheb_half).astype(jnp.bfloat16).astype(jnp.float32)
        return carry

    lax.fori_loop(0, rows_all // (2 * LANES), scale, 0)
    start_sums(table, total, potential, owned, face_count)
    apply_cells(table, total, kinetic, index, slots, held, product, places, sems)
    give_ghosts(total, owned, ghost_out)
    copy_rows(total, sums, 2 * owned)


def last_kernel(width, given, states, returned, face, filtered, total, held):
    owned = filtered.shape[1]
    copy_rows(given, total, 2 * owned)
    add_returned(total, returned, face, held)

    def one(tile, carry):
        start = tile_start(tile)
        nodes = pl.ds(pl.multiple_of(tile * LANES, LANES), LANES)
        low = (2.0 * total[even(start), :] / cheb_half).T
        high = (2.0 * total[even(start + 1), :] / cheb_half).T[: width - LANES, :]
        filtered[:LANES, nodes] = (low - states[:LANES, nodes].astype(jnp.float32)).astype(filtered.dtype)
        filtered[LANES:width, nodes] = (high - states[LANES:width, nodes].astype(jnp.float32)).astype(filtered.dtype)
        return carry

    lax.fori_loop(0, owned // LANES, one, 0, unroll=2)


def filter_states(states, kinetic, potential, cell_nodes, face_map):
    width, owned = states.shape
    cells, slots = cell_nodes.shape
    face_count = face_map.shape[0]
    depth = -(-slots // 16) * 16
    f32 = jnp.float32
    face = 2 * face_map
    index = jnp.pad(2 * cell_nodes, ((0, 0), (0, 384 - slots))).reshape(-1, GROUP, 384)
    potential = potential.reshape(-1, LANES)
    kinetic = jnp.pad(kinetic, ((0, depth - slots), (0, depth - slots)))
    rows_all = 2 * (owned + face_count)
    field = jax.ShapeDtypeStruct((rows_all, LANES), f32)
    sums = jax.ShapeDtypeStruct((packed_rows(face_count), LANES), f32)
    table = VMEM((rows_all, LANES), f32)
    faces_held = VMEM((2, 2 * LANES, LANES), f32)
    work = [
        VMEM((2, 2 * depth, LANES), f32), VMEM((2, 2 * depth, LANES), f32),
        SMEM((2, GROUP, 384), jnp.int32), pltpu.SemaphoreType.DMA((2,)),
    ]
    params = pltpu.CompilerParams(vmem_limit_bytes=LIMIT)

    faces = pl.pallas_call(
        functools.partial(faces_kernel, width),
        name="gather_faces",
        out_shape=jax.ShapeDtypeStruct(sums.shape, states.dtype),
        in_specs=[block(VMEM), block(SMEM)],
        out_specs=block(VMEM),
        scratch_shapes=[VMEM((2 * owned, LANES), f32), faces_held],
        compiler_params=params,
    )(states, face)
    ghosts = passed_along(faces, "brick", -1)
    first, ghost_part, face_part = pl.pallas_call(
        functools.partial(first_kernel, width, slots),
        name="first_apply",
        out_shape=(field, sums, sums),
        in_specs=[block(VMEM)] * 4 + [block(pl.ANY), block(SMEM)],
        out_specs=(block(VMEM),) * 3,
        scratch_shapes=[table, table] + work,
        compiler_params=params,
    )(states, ghosts, potential, kinetic, index, face)
    returned = passed_along(ghost_part, "brick", 1)
    ghost_sums = passed_along(face_part, "brick", -1)
    second, ghost_part = pl.pallas_call(
        functools.partial(second_kernel, owned, slots),
        name="second_apply",
        out_shape=(jax.ShapeDtypeStruct((2 * owned, LANES), f32), sums),
        in_specs=[block(VMEM)] * 5 + [block(pl.ANY), block(SMEM)],
        out_specs=(block(VMEM),) * 2,
        scratch_shapes=[table, table] + work,
        compiler_params=params,
    )(first, returned, ghost_sums, potential, kinetic, index, face)
    returned = passed_along(ghost_part, "brick", 1)
    return pl.pallas_call(
        functools.partial(last_kernel, width),
        name="finish_filter",
        out_shape=jax.ShapeDtypeStruct((width, owned), jnp.bfloat16),
        in_specs=[block(VMEM)] * 3 + [block(SMEM)],
        out_specs=block(VMEM),
        scratch_shapes=[VMEM((2 * owned, LANES), f32), faces_held],
        compiler_params=params,
    )(second, states, returned, face)


X_SIZE, Y_SIZE, Z_SIZE = 4, 4, 8
PLANE = X_SIZE * Y_SIZE
MESH = pl.DeviceIdType.MESH
EXACT = lax.Precision.HIGHEST
CHUNK = 768


def across(left, right):
    return lax.dot_general(left, right, (((1,), (1,)), ((), ())), preferred_element_type=jnp.float32)


def product_of(left, right):
    return jnp.dot(left, right, precision=EXACT, preferred_element_type=jnp.float32)


def unpack(packed):
    corner = packed[128:192, :]
    right = jnp.concatenate([corner.T, packed[288:352, 64:128]], axis=0)
    square = jnp.concatenate([packed[:192, :], right], axis=1)
    mixed = jnp.concatenate([packed[192:288, :], packed[288:384, :64]], axis=1)
    return square, mixed


def root_kernel(
    own, every, root_rows,
    share, inbox, part, levels, own_all, other_all, square, mixed, current, inverse,
    state_sems, here_sem, send_sems, plane_sems, level_sems, gather_sems, pair_sems,
):
    brick, side = lax.axis_index("brick"), lax.axis_index("state")
    width, owned = own.shape
    half = width // 2
    y, z, x = brick % Y_SIZE, (brick // Y_SIZE) % Z_SIZE, brick // (Y_SIZE * Z_SIZE)
    place = x * Y_SIZE + y

    def in_plane(step):
        target = (place + step) % PLANE
        return target, ((target // Y_SIZE) * Z_SIZE + z) * Y_SIZE + target % Y_SIZE

    def in_line(step):
        return (x * Z_SIZE + (z + step) % Z_SIZE) * Y_SIZE + y

    barrier = pltpu.get_barrier_semaphore()
    pl.semaphore_signal(barrier, inc=1, device_id=(brick, 1 - side), device_id_type=MESH)
    for step in range(1, PLANE):
        pl.semaphore_signal(barrier, inc=1, device_id=(in_plane(step)[1], side), device_id_type=MESH)
    for step in range(1, Z_SIZE):
        pl.semaphore_signal(barrier, inc=1, device_id=(in_line(step), side), device_id_type=MESH)
    pl.semaphore_wait(barrier, PLANE + Z_SIZE - 1)

    pieces = 3
    piece = owned // pieces
    place_here = pl.ds(pl.multiple_of(side * width, 16), width)
    here = pltpu.make_async_copy(own, every.at[place_here, :], here_sem)
    here.start()
    states = []
    for number in range(pieces):
        columns = pl.ds(number * piece, piece)
        copy = pltpu.make_async_remote_copy(
            src_ref=own.at[:, columns], dst_ref=every.at[place_here, columns],
            send_sem=state_sems.at[0, number], recv_sem=state_sems.at[1, number],
            device_id=(brick, 1 - side), device_id_type=MESH,
        )
        copy.start()
        states.append(copy)

    square[...] = jnp.zeros_like(square)
    mixed[...] = jnp.zeros_like(mixed)

    def add_square(number, carry):
        values = own[:, pl.ds(pl.multiple_of(number * CHUNK, CHUNK), CHUNK)]
        square[...] += across(values, values)
        return carry

    lax.fori_loop(0, owned // CHUNK, add_square, 0)
    here.wait()
    some = pl.ds(pl.multiple_of(side * half, 16), half)
    for number, copy in enumerate(states):
        copy.wait()

        def add_mixed(step, carry):
            columns = pl.ds(pl.multiple_of(number * piece + step * CHUNK, CHUNK), CHUNK)
            mixed[...] += across(every[some, columns], every[width:, columns])
            return carry

        lax.fori_loop(0, piece // CHUNK, add_mixed, 0)

    share[:192, :] = square[:, :128]
    share[192:288, :] = mixed[:, :128]
    share[288:352, :] = jnp.concatenate([mixed[:64, 128:], square[128:, 128:]], axis=1)
    share[352:384, :] = jnp.concatenate([mixed[64:, 128:], jnp.zeros((32, 64), jnp.float32)], axis=1)

    rows = share.shape[0] // PLANE
    copies = []
    for step in range(1, PLANE):
        target, chip = in_plane(step)
        copy = pltpu.make_async_remote_copy(
            src_ref=share.at[pl.ds(pl.multiple_of(target * rows, 8), rows), :], dst_ref=inbox.at[step - 1],
            send_sem=send_sems.at[step - 1], recv_sem=plane_sems.at[step - 1],
            device_id=(chip, side), device_id_type=MESH,
        )
        copy.start()
        copies.append(copy)
    value = share[pl.ds(pl.multiple_of(place * rows, 8), rows), :]
    for copy in copies:
        copy.wait()
    for step in range(PLANE - 1):
        value = value + inbox[step]
    part[...] = value
    levels[z] = value
    copies = []
    for step in range(1, Z_SIZE):
        copy = pltpu.make_async_remote_copy(
            src_ref=part, dst_ref=levels.at[z],
            send_sem=send_sems.at[PLANE - 2 + step], recv_sem=level_sems.at[step - 1],
            device_id=(in_line(step), side), device_id_type=MESH,
        )
        copy.start()
        copies.append(copy)
    for copy in copies:
        copy.wait()
    value = levels[0]
    for step in range(1, Z_SIZE):
        value = value + levels[step]
    own_all[place] = value
    copies = []
    for step in range(1, PLANE):
        copy = pltpu.make_async_remote_copy(
            src_ref=own_all.at[place], dst_ref=own_all.at[place],
            send_sem=send_sems.at[PLANE + Z_SIZE - 3 + step], recv_sem=gather_sems.at[step - 1],
            device_id=(in_plane(step)[1], side), device_id_type=MESH,
        )
        copy.start()
        copies.append(copy)
    for copy in copies:
        copy.wait()
    swap = pltpu.make_async_remote_copy(
        src_ref=own_all, dst_ref=other_all, send_sem=pair_sems.at[0], recv_sem=pair_sems.at[1],
        device_id=(brick, 1 - side), device_id_type=MESH,
    )
    swap.start()
    swap.wait()

    mine = own_all[...].reshape(PLANE * rows, 128)
    theirs = other_all[...].reshape(PLANE * rows, 128)
    first, first_mixed = unpack(jnp.where(side == 0, mine, theirs))
    second, second_mixed = unpack(jnp.where(side == 0, theirs, mine))
    both = jnp.concatenate([first_mixed, second_mixed], axis=0)
    margin = jnp.concatenate(
        [jnp.concatenate([first, both], axis=1), jnp.concatenate([both.T, second], axis=1)], axis=0
    )
    scale = jnp.sqrt(jnp.sum(margin * margin, axis=(0, 1), keepdims=True) + epsilon)
    total = margin.shape[0]
    row_ids = lax.broadcasted_iota(jnp.int32, (total, total), 0)
    column_ids = lax.broadcasted_iota(jnp.int32, (total, total), 1)
    three = jnp.where(row_ids == column_ids, 3.0, 0.0)
    start = margin / scale
    factor = three - start
    current[...] = 0.5 * product_of(factor, start)
    inverse[...] = 0.5 * factor
    for step in range(1, NS_STEPS - 1):
        factor = three - product_of(inverse[...], current[...])
        current[...] = 0.5 * product_of(factor, current[...])
        inverse[...] = 0.5 * product_of(factor, inverse[...])
    mine = pl.ds(pl.multiple_of(side * width, 8), width)
    row_ids = lax.broadcasted_iota(jnp.int32, (width, total), 0) + side * width
    column_ids = lax.broadcasted_iota(jnp.int32, (width, total), 1)
    factor = jnp.where(row_ids == column_ids, 3.0, 0.0) - product_of(inverse[mine, :], current[...])
    root_rows[...] = (0.5 * product_of(factor, inverse[...])).astype(root_rows.dtype)


def inverse_root(filtered):
    width, owned = filtered.shape
    f32 = jnp.float32
    rows = 384 // PLANE
    dma = pltpu.SemaphoreType.DMA
    return pl.pallas_call(
        root_kernel,
        name="inverse_root",
        out_shape=(
            jax.ShapeDtypeStruct((2 * width, owned), filtered.dtype),
            jax.ShapeDtypeStruct((width, 2 * width), jnp.bfloat16),
        ),
        in_specs=[block(VMEM)],
        out_specs=(block(VMEM),) * 2,
        scratch_shapes=[
            VMEM((384, 128), f32), VMEM((PLANE - 1, rows, 128), f32), VMEM((rows, 128), f32),
            VMEM((Z_SIZE, rows, 128), f32), VMEM((PLANE, rows, 128), f32), VMEM((PLANE, rows, 128), f32),
            VMEM((width, width), f32), VMEM((width // 2, width), f32),
            VMEM((2 * width, 2 * width), f32), VMEM((2 * width, 2 * width), f32),
            dma((2, 3)), dma, dma((2 * PLANE + Z_SIZE - 3,)), dma((PLANE - 1,)), dma((Z_SIZE - 1,)),
            dma((PLANE - 1,)), dma((2,)),
        ],
        compiler_params=pltpu.CompilerParams(
            collective_id=0, has_side_effects=True, vmem_limit_bytes=32 << 20
        ),
    )(filtered)


def local(states, kinetic, potential, cell_nodes, face_map):
    filtered = filter_states(states, kinetic, potential, cell_nodes, face_map)
    every, root_rows = inverse_root(filtered)
    return jnp.dot(root_rows, every, preferred_element_type=jnp.float32)


def solution(mesh):
    in_specs = (P("state", "brick"), P(), P("brick"), P("brick", None), P("brick"))
    out_specs = P("state", "brick")
    return jax.shard_map(local, mesh=mesh, in_specs=in_specs, out_specs=out_specs, check_vma=False)
```

```python
import functools

import jax
import jax.numpy as jnp
from jax import lax
from jax.experimental import pallas as pl
from jax.experimental.pallas import tpu as pltpu
from jax.sharding import PartitionSpec as P

NS_STEPS = 3
LANES = 128
BATCH = 24
GROUP = 4
LIMIT = 20 << 20

cheb_center = 3.0
cheb_half = 7.0
epsilon = 1e-06

VMEM = pltpu.VMEM
SMEM = pltpu.SMEM


def block(space):
    return pl.BlockSpec(memory_space=space)


def passed_along(value, axis, steps):
    count = lax.axis_size(axis)
    pairs = [(source, (source + steps) % count) for source in range(count)]
    return lax.ppermute(value, axis, pairs)


def even(start):
    return pl.ds(start, LANES, stride=2)


def tile_start(tile):
    return pl.multiple_of(tile * (2 * LANES), 2 * LANES)


def padded(value):
    return jnp.concatenate([value, jnp.zeros((value.shape[0], LANES - value.shape[1]), value.dtype)], axis=1)


def packed_rows(faces):
    return faces * 3 // 2


def pack(out, tile, low, high):
    faces = out.shape[0] * 2 // 3
    lane = lax.broadcasted_iota(jnp.int32, (LANES // 2, LANES), 1)
    joined = jnp.where(lane < LANES // 2, high[: LANES // 2], pltpu.roll(high[LANES // 2 :], LANES // 2, axis=1))
    out[tile * LANES : (tile + 1) * LANES, :] = low.astype(out.dtype)
    out[faces + tile * LANES // 2 : faces + (tile + 1) * LANES // 2, :] = joined.astype(out.dtype)


def unpack_rows(ref, tile):
    faces = ref.shape[0] * 2 // 3
    low = ref[tile * LANES : (tile + 1) * LANES, :].astype(jnp.float32)
    joined = ref[faces + tile * LANES // 2 : faces + (tile + 1) * LANES // 2, :].astype(jnp.float32)
    return low, jnp.concatenate([joined, pltpu.roll(joined, LANES // 2, axis=1)], axis=0)


def pair_row(ref, row):
    return ref[pl.ds(row, 2), :]


def gather_rows(source, target, places):
    for row, place in enumerate(places):
        target[2 * row : 2 * row + 2, :] = pair_row(source, place())


def add_rows(total, addend, places):
    for first in range(0, len(places), BATCH):
        rows = range(first, min(first + BATCH, len(places)))
        at = [places[row]() for row in rows]
        sums = [pair_row(total, place) + addend[2 * row : 2 * row + 2, :] for place, row in zip(at, rows)]
        for place, value in zip(at, sums):
            total[pl.ds(place, 2), :] = value


def entries(index, count, *lead):
    start = lead[-1] if lead else 0
    return [functools.partial(lambda i: index[i], start + row) for row in range(count)]


def gather_faces(source, held, face, out):
    for tile in range(face.shape[0] // LANES):
        buffer = held.at[tile % 2]
        gather_rows(source, buffer, entries(face, LANES, tile * LANES))
        pack(out, tile, buffer[even(0), :], buffer[even(1), :])


def fill_table(width, states, table):
    rows = lax.broadcasted_iota(jnp.int32, (LANES, LANES), 0)
    columns = lax.broadcasted_iota(jnp.int32, (LANES, LANES), 1)
    identity = jnp.where(rows == columns, 1.0, 0.0).astype(states.dtype)

    def one(tile, carry):
        nodes = pl.ds(pl.multiple_of(tile * LANES, LANES), LANES)
        values = jnp.concatenate(
            [states[:, nodes], jnp.zeros((2 * LANES - width, LANES), states.dtype)], axis=0
        )
        turned = lax.dot_general(
            identity, values, (((1,), (1,)), ((), ())), preferred_element_type=jnp.float32
        )
        start = tile_start(tile)
        table[even(start), :] = turned[:, :LANES]
        table[even(start + 1), :] = turned[:, LANES:]
        return carry

    lax.fori_loop(0, states.shape[1] // LANES, one, 0, unroll=3)


def spread_kernel(potential, factor):
    def one(tile, carry):
        value = jnp.broadcast_to(potential[pl.ds(tile, 1), :], (LANES, LANES)).T - cheb_center
        start = tile_start(tile)
        factor[even(start), :] = value
        factor[even(start + 1), :] = value
        return carry

    lax.fori_loop(0, potential.shape[0], one, 0)


def copy_rows(source, target, count):
    def take(tile, carry):
        rows = pl.ds(tile_start(tile), 2 * LANES)
        target[rows, :] = source[rows, :]
        return carry

    lax.fori_loop(0, count // (2 * LANES), take, 0)


def faces_kernel(width, states, face, faces, table, held):
    fill_table(width, states, table)
    gather_faces(table, held, face, faces)


def start_sums(table, total, factor, owned, ghosts):
    def one(tile, carry):
        rows = pl.ds(pl.multiple_of(tile * LANES, LANES), LANES)
        total[rows, :] = factor[rows, :] * table[rows, :]
        return carry

    lax.fori_loop(0, 2 * owned // LANES, one, 0, unroll=2)
    total[2 * owned :, :] = jnp.zeros((2 * ghosts, LANES), jnp.float32)


def apply_cells(table, total, kinetic, index, slots, held, product, places, sems):
    depth = kinetic.shape[0]
    groups, cells, _ = index.shape
    for side in range(2):
        held[side, 2 * slots :, :] = jnp.zeros((2 * (depth - slots), LANES), jnp.float32)

    def fetch(group, side):
        return pltpu.make_async_copy(index.at[group], places.at[side], sems.at[side])

    def one_group(group, side):
        fetch(group, side).wait()
        fetch(jnp.minimum(group + 1, groups - 1), 1 - side).start()
        for cell in range(cells):
            at = [functools.partial(lambda i: places[side, cell, i], row) for row in range(slots)]
            values, result = held.at[cell % 2], product.at[cell % 2]
            gather_rows(table, values, at)
            operand = jnp.concatenate(
                [values[pl.ds(0, depth, stride=2), :], values[pl.ds(1, depth, stride=2), :]], axis=1
            ).astype(jnp.bfloat16)
            answer = jnp.dot(kinetic[...], operand, preferred_element_type=jnp.float32)
            result[pl.ds(0, depth, stride=2), :] = answer[:, :LANES]
            result[pl.ds(1, depth, stride=2), :] = answer[:, LANES:]
            add_rows(total, result, at)

    fetch(0, 0).start()

    def two_groups(step, carry):
        one_group(2 * step, 0)
        one_group(2 * step + 1, 1)
        return carry

    lax.fori_loop(0, groups // 2, two_groups, 0)
    fetch(groups - 1, groups % 2).wait()


def give_ghosts(total, owned, out):
    for tile in range(out.shape[0] * 2 // 3 // LANES):
        start = 2 * owned + tile * 2 * LANES
        pack(out, tile, total[even(start), :], total[even(start + 1), :])


def first_kernel(
    width, slots, states, ghosts, potential, kinetic, index, face, sums, ghost_out, face_out,
    table, total, held, product, places, sems,
):
    owned = states.shape[1]
    face_count = face.shape[0]
    fill_table(width, states, table)
    for tile in range(face_count // LANES):
        start = 2 * owned + tile * 2 * LANES
        low, high = unpack_rows(ghosts, tile)
        table[even(start), :] = low
        table[even(start + 1), :] = high
    start_sums(table, total, potential, owned, face_count)
    apply_cells(table, total, kinetic, index, slots, held, product, places, sems)
    give_ghosts(total, owned, ghost_out)
    gather_faces(total, held, face, face_out)
    copy_rows(total, sums, total.shape[0])


def add_returned(total, returned, face, held):
    for tile in range(face.shape[0] // LANES):
        low, high = unpack_rows(returned, tile)
        buffer = held.at[tile % 2]
        buffer[even(0), :] = low
        buffer[even(1), :] = high
        add_rows(total, buffer, entries(face, LANES, tile * LANES))


def second_kernel(
    owned, slots, given, returned, ghost_sums, potential, kinetic, index, face, sums, ghost_out,
    table, total, held, product, places, sems,
):
    face_count = face.shape[0]
    rows_all = table.shape[0]
    copy_rows(given, table, rows_all)
    add_returned(table, returned, face, held)
    for tile in range(face_count // LANES):
        start = 2 * owned + tile * 2 * LANES
        low, high = unpack_rows(ghost_sums, tile)
        table[even(start), :] = table[even(start), :] + low
        table[even(start + 1), :] = table[even(start + 1), :] + high

    def scale(tile, carry):
        rows = pl.ds(tile_start(tile), 2 * LANES)
        table[rows, :] = (table[rows, :] / cheb_half).astype(jnp.bfloat16).astype(jnp.float32)
        return carry

    lax.fori_loop(0, rows_all // (2 * LANES), scale, 0)
    start_sums(table, total, potential, owned, face_count)
    apply_cells(table, total, kinetic, index, slots, held, product, places, sems)
    give_ghosts(total, owned, ghost_out)
    copy_rows(total, sums, 2 * owned)


def last_kernel(width, given, states, returned, face, filtered, total, held):
    owned = filtered.shape[1]
    copy_rows(given, total, 2 * owned)
    add_returned(total, returned, face, held)

    def one(tile, carry):
        start = tile_start(tile)
        nodes = pl.ds(pl.multiple_of(tile * LANES, LANES), LANES)
        low = (2.0 * total[even(start), :] / cheb_half).T
        high = (2.0 * total[even(start + 1), :] / cheb_half).T[: width - LANES, :]
        filtered[:LANES, nodes] = (low - states[:LANES, nodes].astype(jnp.float32)).astype(filtered.dtype)
        filtered[LANES:width, nodes] = (high - states[LANES:width, nodes].astype(jnp.float32)).astype(filtered.dtype)
        return carry

    lax.fori_loop(0, owned // LANES, one, 0, unroll=2)


def filter_states(states, kinetic, potential, cell_nodes, face_map):
    width, owned = states.shape
    cells, slots = cell_nodes.shape
    face_count = face_map.shape[0]
    depth = -(-slots // 16) * 16
    f32 = jnp.float32
    face = 2 * face_map
    index = jnp.pad(2 * cell_nodes, ((0, 0), (0, 384 - slots))).reshape(-1, GROUP, 384)
    potential = pl.pallas_call(
        spread_kernel,
        name="spread_potential",
        out_shape=jax.ShapeDtypeStruct((2 * owned, LANES), f32),
        in_specs=[block(VMEM)],
        out_specs=block(VMEM),
        compiler_params=pltpu.CompilerParams(vmem_limit_bytes=LIMIT),
        cost_estimate=pl.CostEstimate(flops=2 * owned * LANES, bytes_accessed=24 * owned * LANES, transcendentals=0),
    )(potential.reshape(-1, LANES))
    kinetic = jnp.pad(kinetic, ((0, depth - slots), (0, depth - slots)))
    rows_all = 2 * (owned + face_count)
    field = jax.ShapeDtypeStruct((rows_all, LANES), f32)
    sums = jax.ShapeDtypeStruct((packed_rows(face_count), LANES), f32)
    table = VMEM((rows_all, LANES), f32)
    faces_held = VMEM((2, 2 * LANES, LANES), f32)
    work = [
        VMEM((2, 2 * depth, LANES), f32), VMEM((2, 2 * depth, LANES), f32),
        SMEM((2, GROUP, 384), jnp.int32), pltpu.SemaphoreType.DMA((2,)),
    ]
    params = pltpu.CompilerParams(vmem_limit_bytes=LIMIT)

    faces = pl.pallas_call(
        functools.partial(faces_kernel, width),
        name="gather_faces",
        out_shape=jax.ShapeDtypeStruct(sums.shape, states.dtype),
        in_specs=[block(VMEM), block(SMEM)],
        out_specs=block(VMEM),
        scratch_shapes=[VMEM((2 * owned, LANES), f32), faces_held],
        compiler_params=params,
    )(states, face)
    ghosts = passed_along(faces, "brick", -1)
    first, ghost_part, face_part = pl.pallas_call(
        functools.partial(first_kernel, width, slots),
        name="first_apply",
        out_shape=(field, sums, sums),
        in_specs=[block(VMEM)] * 4 + [block(pl.ANY), block(SMEM)],
        out_specs=(block(VMEM),) * 3,
        scratch_shapes=[table, table] + work,
        compiler_params=params,
    )(states, ghosts, potential, kinetic, index, face)
    returned = passed_along(ghost_part, "brick", 1)
    ghost_sums = passed_along(face_part, "brick", -1)
    second, ghost_part = pl.pallas_call(
        functools.partial(second_kernel, owned, slots),
        name="second_apply",
        out_shape=(jax.ShapeDtypeStruct((2 * owned, LANES), f32), sums),
        in_specs=[block(VMEM)] * 5 + [block(pl.ANY), block(SMEM)],
        out_specs=(block(VMEM),) * 2,
        scratch_shapes=[table, table] + work,
        compiler_params=params,
    )(first, returned, ghost_sums, potential, kinetic, index, face)
    returned = passed_along(ghost_part, "brick", 1)
    return pl.pallas_call(
        functools.partial(last_kernel, width),
        name="finish_filter",
        out_shape=jax.ShapeDtypeStruct((width, owned), jnp.bfloat16),
        in_specs=[block(VMEM)] * 3 + [block(SMEM)],
        out_specs=block(VMEM),
        scratch_shapes=[VMEM((2 * owned, LANES), f32), faces_held],
        compiler_params=params,
    )(second, states, returned, face)


X_SIZE, Y_SIZE, Z_SIZE = 4, 4, 8
PLANE = X_SIZE * Y_SIZE
MESH = pl.DeviceIdType.MESH
EXACT = lax.Precision.HIGHEST
CHUNK = 768


def across(left, right):
    return lax.dot_general(left, right, (((1,), (1,)), ((), ())), preferred_element_type=jnp.float32)


def product_of(left, right):
    return jnp.dot(left, right, precision=EXACT, preferred_element_type=jnp.float32)


def unpack(packed):
    corner = packed[128:192, :]
    right = jnp.concatenate([corner.T, packed[288:352, 64:128]], axis=0)
    square = jnp.concatenate([packed[:192, :], right], axis=1)
    mixed = jnp.concatenate([packed[192:288, :], packed[288:384, :64]], axis=1)
    return square, mixed


def root_kernel(
    own, every, root_rows,
    share, inbox, part, levels, own_all, other_all, square, mixed, current, inverse,
    state_sems, here_sem, send_sems, plane_sems, level_sems, gather_sems, pair_sems,
):
    brick, side = lax.axis_index("brick"), lax.axis_index("state")
    width, owned = own.shape
    half = width // 2
    y, z, x = brick % Y_SIZE, (brick // Y_SIZE) % Z_SIZE, brick // (Y_SIZE * Z_SIZE)
    place = x * Y_SIZE + y

    def in_plane(step):
        target = (place + step) % PLANE
        return target, ((target // Y_SIZE) * Z_SIZE + z) * Y_SIZE + target % Y_SIZE

    def in_line(step):
        return (x * Z_SIZE + (z + step) % Z_SIZE) * Y_SIZE + y

    barrier = pltpu.get_barrier_semaphore()
    pl.semaphore_signal(barrier, inc=1, device_id=(brick, 1 - side), device_id_type=MESH)
    for step in range(1, PLANE):
        pl.semaphore_signal(barrier, inc=1, device_id=(in_plane(step)[1], side), device_id_type=MESH)
    for step in range(1, Z_SIZE):
        pl.semaphore_signal(barrier, inc=1, device_id=(in_line(step), side), device_id_type=MESH)
    pl.semaphore_wait(barrier, PLANE + Z_SIZE - 1)

    pieces = 3
    piece = owned // pieces
    place_here = pl.ds(pl.multiple_of(side * width, 16), width)
    here = pltpu.make_async_copy(own, every.at[place_here, :], here_sem)
    here.start()
    states = []
    for number in range(pieces):
        columns = pl.ds(number * piece, piece)
        copy = pltpu.make_async_remote_copy(
            src_ref=own.at[:, columns], dst_ref=every.at[place_here, columns],
            send_sem=state_sems.at[0, number], recv_sem=state_sems.at[1, number],
            device_id=(brick, 1 - side), device_id_type=MESH,
        )
        copy.start()
        states.append(copy)

    square[...] = jnp.zeros_like(square)
    mixed[...] = jnp.zeros_like(mixed)

    def add_square(number, carry):
        values = own[:, pl.ds(pl.multiple_of(number * CHUNK, CHUNK), CHUNK)]
        square[...] += across(values, values)
        return carry

    lax.fori_loop(0, owned // CHUNK, add_square, 0)
    here.wait()
    some = pl.ds(pl.multiple_of(side * half, 16), half)
    for number, copy in enumerate(states):
        copy.wait()

        def add_mixed(step, carry):
            columns = pl.ds(pl.multiple_of(number * piece + step * CHUNK, CHUNK), CHUNK)
            mixed[...] += across(every[some, columns], every[width:, columns])
            return carry

        lax.fori_loop(0, piece // CHUNK, add_mixed, 0)

    share[:192, :] = square[:, :128]
    share[192:288, :] = mixed[:, :128]
    share[288:352, :] = jnp.concatenate([mixed[:64, 128:], square[128:, 128:]], axis=1)
    share[352:384, :] = jnp.concatenate([mixed[64:, 128:], jnp.zeros((32, 64), jnp.float32)], axis=1)

    rows = share.shape[0] // PLANE
    copies = []
    for step in range(1, PLANE):
        target, chip = in_plane(step)
        copy = pltpu.make_async_remote_copy(
            src_ref=share.at[pl.ds(pl.multiple_of(target * rows, 8), rows), :], dst_ref=inbox.at[step - 1],
            send_sem=send_sems.at[step - 1], recv_sem=plane_sems.at[step - 1],
            device_id=(chip, side), device_id_type=MESH,
        )
        copy.start()
        copies.append(copy)
    value = share[pl.ds(pl.multiple_of(place * rows, 8), rows), :]
    for copy in copies:
        copy.wait()
    for step in range(PLANE - 1):
        value = value + inbox[step]
    part[...] = value
    levels[z] = value
    copies = []
    for step in range(1, Z_SIZE):
        copy = pltpu.make_async_remote_copy(
            src_ref=part, dst_ref=levels.at[z],
            send_sem=send_sems.at[PLANE - 2 + step], recv_sem=level_sems.at[step - 1],
            device_id=(in_line(step), side), device_id_type=MESH,
        )
        copy.start()
        copies.append(copy)
    for copy in copies:
        copy.wait()
    value = levels[0]
    for step in range(1, Z_SIZE):
        value = value + levels[step]
    own_all[place] = value
    copies = []
    for step in range(1, PLANE):
        copy = pltpu.make_async_remote_copy(
            src_ref=own_all.at[place], dst_ref=own_all.at[place],
            send_sem=send_sems.at[PLANE + Z_SIZE - 3 + step], recv_sem=gather_sems.at[step - 1],
            device_id=(in_plane(step)[1], side), device_id_type=MESH,
        )
        copy.start()
        copies.append(copy)
    for copy in copies:
        copy.wait()
    swap = pltpu.make_async_remote_copy(
        src_ref=own_all, dst_ref=other_all, send_sem=pair_sems.at[0], recv_sem=pair_sems.at[1],
        device_id=(brick, 1 - side), device_id_type=MESH,
    )
    swap.start()
    swap.wait()

    mine = own_all[...].reshape(PLANE * rows, 128)
    theirs = other_all[...].reshape(PLANE * rows, 128)
    first, first_mixed = unpack(jnp.where(side == 0, mine, theirs))
    second, second_mixed = unpack(jnp.where(side == 0, theirs, mine))
    both = jnp.concatenate([first_mixed, second_mixed], axis=0)
    margin = jnp.concatenate(
        [jnp.concatenate([first, both], axis=1), jnp.concatenate([both.T, second], axis=1)], axis=0
    )
    scale = jnp.sqrt(jnp.sum(margin * margin, axis=(0, 1), keepdims=True) + epsilon)
    total = margin.shape[0]
    row_ids = lax.broadcasted_iota(jnp.int32, (total, total), 0)
    column_ids = lax.broadcasted_iota(jnp.int32, (total, total), 1)
    three = jnp.where(row_ids == column_ids, 3.0, 0.0)
    start = margin / scale
    factor = three - start
    current[...] = 0.5 * product_of(factor, start)
    inverse[...] = 0.5 * factor
    for step in range(1, NS_STEPS - 1):
        factor = three - product_of(inverse[...], current[...])
        current[...] = 0.5 * product_of(factor, current[...])
        inverse[...] = 0.5 * product_of(factor, inverse[...])
    mine = pl.ds(pl.multiple_of(side * width, 8), width)
    row_ids = lax.broadcasted_iota(jnp.int32, (width, total), 0) + side * width
    column_ids = lax.broadcasted_iota(jnp.int32, (width, total), 1)
    factor = jnp.where(row_ids == column_ids, 3.0, 0.0) - product_of(inverse[mine, :], current[...])
    root_rows[...] = (0.5 * product_of(factor, inverse[...])).astype(root_rows.dtype)


def inverse_root(filtered):
    width, owned = filtered.shape
    f32 = jnp.float32
    rows = 384 // PLANE
    dma = pltpu.SemaphoreType.DMA
    return pl.pallas_call(
        root_kernel,
        name="inverse_root",
        out_shape=(
            jax.ShapeDtypeStruct((2 * width, owned), filtered.dtype),
            jax.ShapeDtypeStruct((width, 2 * width), jnp.bfloat16),
        ),
        in_specs=[block(VMEM)],
        out_specs=(block(VMEM),) * 2,
        scratch_shapes=[
            VMEM((384, 128), f32), VMEM((PLANE - 1, rows, 128), f32), VMEM((rows, 128), f32),
            VMEM((Z_SIZE, rows, 128), f32), VMEM((PLANE, rows, 128), f32), VMEM((PLANE, rows, 128), f32),
            VMEM((width, width), f32), VMEM((width // 2, width), f32),
            VMEM((2 * width, 2 * width), f32), VMEM((2 * width, 2 * width), f32),
            dma((2, 3)), dma, dma((2 * PLANE + Z_SIZE - 3,)), dma((PLANE - 1,)), dma((Z_SIZE - 1,)),
            dma((PLANE - 1,)), dma((2,)),
        ],
        compiler_params=pltpu.CompilerParams(
            collective_id=0, has_side_effects=True, vmem_limit_bytes=32 << 20
        ),
    )(filtered)


def local(states, kinetic, potential, cell_nodes, face_map):
    filtered = filter_states(states, kinetic, potential, cell_nodes, face_map)
    every, root_rows = inverse_root(filtered)
    return jnp.dot(root_rows, every, preferred_element_type=jnp.float32)


def solution(mesh):
    in_specs = (P("state", "brick"), P(), P("brick"), P("brick", None), P("brick"))
    out_specs = P("state", "brick")
    return jax.shard_map(local, mesh=mesh, in_specs=in_specs, out_specs=out_specs, check_vma=False)
```

```python
import functools

import jax
import jax.numpy as jnp
from jax import lax
from jax.experimental import pallas as pl
from jax.experimental.pallas import tpu as pltpu
from jax.sharding import PartitionSpec as P

NS_STEPS = 3
LANES = 128
BATCH = 24
GROUP = 4
LIMIT = 20 << 20

cheb_center = 3.0
cheb_half = 7.0
epsilon = 1e-06

VMEM = pltpu.VMEM
SMEM = pltpu.SMEM


def block(space):
    return pl.BlockSpec(memory_space=space)


def passed_along(value, axis, steps):
    count = lax.axis_size(axis)
    pairs = [(source, (source + steps) % count) for source in range(count)]
    return lax.ppermute(value, axis, pairs)


def even(start):
    return pl.ds(start, LANES, stride=2)


def tile_start(tile):
    return pl.multiple_of(tile * (2 * LANES), 2 * LANES)


def padded(value):
    return jnp.concatenate([value, jnp.zeros((value.shape[0], LANES - value.shape[1]), value.dtype)], axis=1)


def packed_rows(faces):
    return faces * 3 // 2


def pack(out, tile, low, high):
    faces = out.shape[0] * 2 // 3
    lane = lax.broadcasted_iota(jnp.int32, (LANES // 2, LANES), 1)
    joined = jnp.where(lane < LANES // 2, high[: LANES // 2], pltpu.roll(high[LANES // 2 :], LANES // 2, axis=1))
    out[tile * LANES : (tile + 1) * LANES, :] = low.astype(out.dtype)
    out[faces + tile * LANES // 2 : faces + (tile + 1) * LANES // 2, :] = joined.astype(out.dtype)


def unpack_rows(ref, tile):
    faces = ref.shape[0] * 2 // 3
    low = ref[tile * LANES : (tile + 1) * LANES, :].astype(jnp.float32)
    joined = ref[faces + tile * LANES // 2 : faces + (tile + 1) * LANES // 2, :].astype(jnp.float32)
    return low, jnp.concatenate([joined, pltpu.roll(joined, LANES // 2, axis=1)], axis=0)


def pair_row(ref, row):
    return ref[pl.ds(row, 2), :]


def gather_rows(source, target, places):
    for row, place in enumerate(places):
        target[2 * row : 2 * row + 2, :] = pair_row(source, place())


def add_rows(total, addend, places):
    for first in range(0, len(places), BATCH):
        rows = range(first, min(first + BATCH, len(places)))
        at = [places[row]() for row in rows]
        sums = [pair_row(total, place) + addend[2 * row : 2 * row + 2, :] for place, row in zip(at, rows)]
        for place, value in zip(at, sums):
            total[pl.ds(place, 2), :] = value


def entries(index, count, *lead):
    start = lead[-1] if lead else 0
    return [functools.partial(lambda i: index[i], start + row) for row in range(count)]


def gather_faces(source, held, face, out):
    for tile in range(face.shape[0] // LANES):
        buffer = held.at[tile % 2]
        gather_rows(source, buffer, entries(face, LANES, tile * LANES))
        pack(out, tile, buffer[even(0), :], buffer[even(1), :])


def fill_table(width, states, table):
    def one(tile, carry):
        nodes = pl.ds(pl.multiple_of(tile * LANES, LANES), LANES)
        low = states[:LANES, nodes].astype(jnp.float32)
        high = states[LANES:width, nodes].astype(jnp.float32)
        high = jnp.concatenate([high, jnp.zeros((2 * LANES - width, LANES), jnp.float32)], axis=0)
        start = tile_start(tile)
        table[even(start), :] = low.T
        table[even(start + 1), :] = high.T
        return carry

    lax.fori_loop(0, states.shape[1] // LANES, one, 0, unroll=2)


def spread_kernel(potential, factor):
    def one(tile, carry):
        value = jnp.broadcast_to(potential[pl.ds(tile, 1), :], (LANES, LANES)).T - cheb_center
        start = tile_start(tile)
        factor[even(start), :] = value
        factor[even(start + 1), :] = value
        return carry

    lax.fori_loop(0, potential.shape[0], one, 0, unroll=2)


def copy_rows(source, target, count):
    def take(tile, carry):
        rows = pl.ds(tile_start(tile), 2 * LANES)
        target[rows, :] = source[rows, :]
        return carry

    lax.fori_loop(0, count // (2 * LANES), take, 0)


def faces_kernel(width, states, face, faces, table, held):
    fill_table(width, states, table)
    gather_faces(table, held, face, faces)


def start_sums(table, total, factor, owned, ghosts):
    def one(tile, carry):
        rows = pl.ds(pl.multiple_of(tile * LANES, LANES), LANES)
        total[rows, :] = factor[rows, :] * table[rows, :]
        return carry

    lax.fori_loop(0, 2 * owned // LANES, one, 0, unroll=2)
    total[2 * owned :, :] = jnp.zeros((2 * ghosts, LANES), jnp.float32)


def apply_cells(table, total, kinetic, index, slots, held, product, places, sems):
    depth = kinetic.shape[0]
    groups, cells, _ = index.shape
    for side in range(2):
        held[side, 2 * slots :, :] = jnp.zeros((2 * (depth - slots), LANES), jnp.float32)

    def fetch(group, side):
        return pltpu.make_async_copy(index.at[group], places.at[side], sems.at[side])

    def one_group(group, side):
        fetch(group, side).wait()
        fetch(jnp.minimum(group + 1, groups - 1), 1 - side).start()
        for cell in range(cells):
            at = [functools.partial(lambda i: places[side, cell, i], row) for row in range(slots)]
            values, result = held.at[cell % 2], product.at[cell % 2]
            gather_rows(table, values, at)
            operand = jnp.concatenate(
                [values[pl.ds(0, depth, stride=2), :], values[pl.ds(1, depth, stride=2), :]], axis=1
            ).astype(jnp.bfloat16)
            answer = jnp.dot(kinetic[...], operand, preferred_element_type=jnp.float32)
            result[pl.ds(0, depth, stride=2), :] = answer[:, :LANES]
            result[pl.ds(1, depth, stride=2), :] = answer[:, LANES:]
            add_rows(total, result, at)

    fetch(0, 0).start()

    def two_groups(step, carry):
        one_group(2 * step, 0)
        one_group(2 * step + 1, 1)
        return carry

    lax.fori_loop(0, groups // 2, two_groups, 0)
    fetch(groups - 1, groups % 2).wait()


def give_ghosts(total, owned, out):
    for tile in range(out.shape[0] * 2 // 3 // LANES):
        start = 2 * owned + tile * 2 * LANES
        pack(out, tile, total[even(start), :], total[even(start + 1), :])


def first_kernel(
    width, slots, states, ghosts, potential, kinetic, index, face, sums, ghost_out, face_out,
    table, total, held, product, places, sems,
):
    owned = states.shape[1]
    face_count = face.shape[0]
    fill_table(width, states, table)
    for tile in range(face_count // LANES):
        start = 2 * owned + tile * 2 * LANES
        low, high = unpack_rows(ghosts, tile)
        table[even(start), :] = low
        table[even(start + 1), :] = high
    start_sums(table, total, potential, owned, face_count)
    apply_cells(table, total, kinetic, index, slots, held, product, places, sems)
    give_ghosts(total, owned, ghost_out)
    gather_faces(total, held, face, face_out)
    copy_rows(total, sums, total.shape[0])


def add_returned(total, returned, face, held):
    for tile in range(face.shape[0] // LANES):
        low, high = unpack_rows(returned, tile)
        buffer = held.at[tile % 2]
        buffer[even(0), :] = low
        buffer[even(1), :] = high
        add_rows(total, buffer, entries(face, LANES, tile * LANES))


def second_kernel(
    owned, slots, given, returned, ghost_sums, potential, kinetic, index, face, sums, ghost_out,
    table, total, held, product, places, sems,
):
    face_count = face.shape[0]
    rows_all = table.shape[0]
    copy_rows(given, table, rows_all)
    add_returned(table, returned, face, held)
    for tile in range(face_count // LANES):
        start = 2 * owned + tile * 2 * LANES
        low, high = unpack_rows(ghost_sums, tile)
        table[even(start), :] = table[even(start), :] + low
        table[even(start + 1), :] = table[even(start + 1), :] + high

    def scale(tile, carry):
        rows = pl.ds(tile_start(tile), 2 * LANES)
        table[rows, :] = (table[rows, :] / cheb_half).astype(jnp.bfloat16).astype(jnp.float32)
        return carry

    lax.fori_loop(0, rows_all // (2 * LANES), scale, 0)
    start_sums(table, total, potential, owned, face_count)
    apply_cells(table, total, kinetic, index, slots, held, product, places, sems)
    give_ghosts(total, owned, ghost_out)
    copy_rows(total, sums, 2 * owned)


def last_kernel(width, given, states, returned, face, filtered, total, held):
    owned = filtered.shape[1]
    copy_rows(given, total, 2 * owned)
    add_returned(total, returned, face, held)

    def one(tile, carry):
        start = tile_start(tile)
        nodes = pl.ds(pl.multiple_of(tile * LANES, LANES), LANES)
        low = (2.0 * total[even(start), :] / cheb_half).T
        high = (2.0 * total[even(start + 1), :] / cheb_half).T[: width - LANES, :]
        filtered[:LANES, nodes] = (low - states[:LANES, nodes].astype(jnp.float32)).astype(filtered.dtype)
        filtered[LANES:width, nodes] = (high - states[LANES:width, nodes].astype(jnp.float32)).astype(filtered.dtype)
        return carry

    lax.fori_loop(0, owned // LANES, one, 0, unroll=2)


def filter_states(states, kinetic, potential, cell_nodes, face_map):
    width, owned = states.shape
    cells, slots = cell_nodes.shape
    face_count = face_map.shape[0]
    depth = -(-slots // 16) * 16
    f32 = jnp.float32
    face = 2 * face_map
    index = jnp.pad(2 * cell_nodes, ((0, 0), (0, 384 - slots))).reshape(-1, GROUP, 384)
    potential = pl.pallas_call(
        spread_kernel,
        name="spread_potential",
        out_shape=jax.ShapeDtypeStruct((2 * owned, LANES), f32),
        in_specs=[block(VMEM)],
        out_specs=block(VMEM),
        compiler_params=pltpu.CompilerParams(vmem_limit_bytes=LIMIT),
        cost_estimate=pl.CostEstimate(flops=2 * owned * LANES, bytes_accessed=24 * owned * LANES, transcendentals=0),
    )(potential.reshape(-1, LANES))
    kinetic = jnp.pad(kinetic, ((0, depth - slots), (0, depth - slots)))
    rows_all = 2 * (owned + face_count)
    field = jax.ShapeDtypeStruct((rows_all, LANES), f32)
    sums = jax.ShapeDtypeStruct((packed_rows(face_count), LANES), f32)
    table = VMEM((rows_all, LANES), f32)
    faces_held = VMEM((2, 2 * LANES, LANES), f32)
    work = [
        VMEM((2, 2 * depth, LANES), f32), VMEM((2, 2 * depth, LANES), f32),
        SMEM((2, GROUP, 384), jnp.int32), pltpu.SemaphoreType.DMA((2,)),
    ]
    params = pltpu.CompilerParams(vmem_limit_bytes=LIMIT)

    faces = pl.pallas_call(
        functools.partial(faces_kernel, width),
        name="gather_faces",
        out_shape=jax.ShapeDtypeStruct(sums.shape, states.dtype),
        in_specs=[block(VMEM), block(SMEM)],
        out_specs=block(VMEM),
        scratch_shapes=[VMEM((2 * owned, LANES), f32), faces_held],
        compiler_params=params,
    )(states, face)
    ghosts = passed_along(faces, "brick", -1)
    first, ghost_part, face_part = pl.pallas_call(
        functools.partial(first_kernel, width, slots),
        name="first_apply",
        out_shape=(field, sums, sums),
        in_specs=[block(VMEM)] * 4 + [block(pl.ANY), block(SMEM)],
        out_specs=(block(VMEM),) * 3,
        scratch_shapes=[table, table] + work,
        compiler_params=params,
    )(states, ghosts, potential, kinetic, index, face)
    returned = passed_along(ghost_part, "brick", 1)
    ghost_sums = passed_along(face_part, "brick", -1)
    second, ghost_part = pl.pallas_call(
        functools.partial(second_kernel, owned, slots),
        name="second_apply",
        out_shape=(jax.ShapeDtypeStruct((2 * owned, LANES), f32), sums),
        in_specs=[block(VMEM)] * 5 + [block(pl.ANY), block(SMEM)],
        out_specs=(block(VMEM),) * 2,
        scratch_shapes=[table, table] + work,
        compiler_params=params,
    )(first, returned, ghost_sums, potential, kinetic, index, face)
    returned = passed_along(ghost_part, "brick", 1)
    return pl.pallas_call(
        functools.partial(last_kernel, width),
        name="finish_filter",
        out_shape=jax.ShapeDtypeStruct((width, owned), jnp.bfloat16),
        in_specs=[block(VMEM)] * 3 + [block(SMEM)],
        out_specs=block(VMEM),
        scratch_shapes=[VMEM((2 * owned, LANES), f32), faces_held],
        compiler_params=params,
    )(second, states, returned, face)


X_SIZE, Y_SIZE, Z_SIZE = 4, 4, 8
PLANE = X_SIZE * Y_SIZE
MESH = pl.DeviceIdType.MESH


def across(left, right):
    return lax.dot_general(left, right, (((1,), (1,)), ((), ())), preferred_element_type=jnp.float32)


LEFT_PARTS = (2, 0, 1, 1, 0, 0)
RIGHT_PARTS = (0, 2, 1, 0, 1, 0)


def parts_of(value):
    high = value.astype(jnp.bfloat16)
    rest = value - high.astype(jnp.float32)
    middle = rest.astype(jnp.bfloat16)
    return high, middle, (rest - middle.astype(jnp.float32)).astype(jnp.bfloat16)


def put_left(ref, value):
    rows, size = value.shape
    parts = parts_of(value)
    for number, part in enumerate(LEFT_PARTS):
        ref[:rows, number * size : (number + 1) * size] = parts[part]


def put_right(ref, value):
    size = value.shape[0]
    parts = parts_of(value)
    for number, part in enumerate(RIGHT_PARTS):
        ref[number * size : (number + 1) * size, :] = parts[part]


def product_of(left, right, rows):
    return jnp.dot(left[:rows, :], right[...], preferred_element_type=jnp.float32)


def three_less(offset, value):
    row_ids = lax.broadcasted_iota(jnp.int32, value.shape, 0) + offset
    column_ids = lax.broadcasted_iota(jnp.int32, value.shape, 1)
    return jnp.where(row_ids == column_ids, 3.0, 0.0) - value


def unpack(packed):
    corner = packed[128:192, :]
    right = jnp.concatenate([corner.T, packed[288:352, 64:128]], axis=0)
    square = jnp.concatenate([packed[:192, :], right], axis=1)
    mixed = jnp.concatenate([packed[192:288, :], packed[288:384, :64]], axis=1)
    return square, mixed


def pack_share(ref, square, mixed, start, half):
    some = mixed[pl.ds(start, half), :]
    ref[:192, :] = square[:, :128]
    ref[192:288, :] = some[:, :128]
    ref[288:352, :] = jnp.concatenate([some[:64, 128:], square[128:, 128:]], axis=1)
    ref[352:384, :] = jnp.concatenate([some[64:, 128:], jnp.zeros((32, 64), jnp.float32)], axis=1)


def root_kernel(
    own, every, root_rows,
    share, inbox, part, levels, own_all, other_all, sent, received, own_sum, other_sum, mixed, current, inverse, factor, left, right,
    state_sems, share_sems, here_sem, send_sems, plane_sems, level_sems, gather_sems, pair_sems,
):
    brick, side = lax.axis_index("brick"), lax.axis_index("state")
    width, owned = own.shape
    half = width // 2
    y, z, x = brick % Y_SIZE, (brick // Y_SIZE) % Z_SIZE, brick // (Y_SIZE * Z_SIZE)
    place = x * Y_SIZE + y

    def in_plane(step):
        target = (place + step) % PLANE
        return target, ((target // Y_SIZE) * Z_SIZE + z) * Y_SIZE + target % Y_SIZE

    def in_line(step):
        return (x * Z_SIZE + (z + step) % Z_SIZE) * Y_SIZE + y

    barrier = pltpu.get_barrier_semaphore()
    pl.semaphore_signal(barrier, inc=1, device_id=(brick, 1 - side), device_id_type=MESH)
    for step in range(1, PLANE):
        pl.semaphore_signal(barrier, inc=1, device_id=(in_plane(step)[1], side), device_id_type=MESH)
    for step in range(1, Z_SIZE):
        pl.semaphore_signal(barrier, inc=1, device_id=(in_line(step), side), device_id_type=MESH)
    pl.semaphore_wait(barrier, PLANE + Z_SIZE - 1)

    pieces = 3
    piece = owned // 2 // pieces
    place_here = pl.ds(pl.multiple_of(side * width, 16), width)
    here = pltpu.make_async_copy(own, every.at[place_here, :], here_sem)
    here.start()

    def columns(part, number):
        return pl.ds(pl.multiple_of(part * (owned // 2) + number * piece, 128), piece)

    def swap_states(part, number, slot):
        some = columns(part, number)
        copy = pltpu.make_async_remote_copy(
            src_ref=own.at[:, some], dst_ref=every.at[place_here, some],
            send_sem=state_sems.at[0, slot], recv_sem=state_sems.at[1, slot],
            device_id=(brick, 1 - side), device_id_type=MESH,
        )
        copy.start()
        return copy

    needed = [swap_states(1 - side, number, number) for number in range(pieces)]
    own_sum[...] = jnp.zeros_like(own_sum)
    for number in range(pieces):
        values = own[:, columns(side, number)]
        own_sum[...] += across(values, values)
    here.wait()
    other_sum[...] = jnp.zeros_like(other_sum)
    mixed[...] = jnp.zeros_like(mixed)
    place_there = pl.ds(pl.multiple_of((1 - side) * width, 16), width)
    for number, copy in enumerate(needed):
        copy.wait()
        some = columns(side, number)
        values = every[place_there, some]
        other_sum[...] += across(values, values)
        mixed[...] += across(every[:width, some], every[width:, some])
    rest = [swap_states(side, number, pieces + number) for number in range(pieces)]

    pack_share(sent, other_sum, mixed, pl.multiple_of((1 - side) * half, 8), half)
    swap = pltpu.make_async_remote_copy(
        src_ref=sent, dst_ref=received, send_sem=share_sems.at[0], recv_sem=share_sems.at[1],
        device_id=(brick, 1 - side), device_id_type=MESH,
    )
    swap.start()
    pack_share(share, own_sum, mixed, pl.multiple_of(side * half, 8), half)
    swap.wait()
    share[...] += received[...]

    rows = share.shape[0] // PLANE
    copies = []
    for step in range(1, PLANE):
        target, chip = in_plane(step)
        copy = pltpu.make_async_remote_copy(
            src_ref=share.at[pl.ds(pl.multiple_of(target * rows, 8), rows), :], dst_ref=inbox.at[step - 1],
            send_sem=send_sems.at[step - 1], recv_sem=plane_sems.at[step - 1],
            device_id=(chip, side), device_id_type=MESH,
        )
        copy.start()
        copies.append(copy)
    value = share[pl.ds(pl.multiple_of(place * rows, 8), rows), :]
    for copy in copies:
        copy.wait()
    for step in range(PLANE - 1):
        value = value + inbox[step]
    part[...] = value
    levels[z] = value
    copies = []
    for step in range(1, Z_SIZE):
        copy = pltpu.make_async_remote_copy(
            src_ref=part, dst_ref=levels.at[z],
            send_sem=send_sems.at[PLANE - 2 + step], recv_sem=level_sems.at[step - 1],
            device_id=(in_line(step), side), device_id_type=MESH,
        )
        copy.start()
        copies.append(copy)
    for copy in copies:
        copy.wait()
    value = levels[0]
    for step in range(1, Z_SIZE):
        value = value + levels[step]
    own_all[place] = value
    copies = []
    for step in range(1, PLANE):
        copy = pltpu.make_async_remote_copy(
            src_ref=own_all.at[place], dst_ref=own_all.at[place],
            send_sem=send_sems.at[PLANE + Z_SIZE - 3 + step], recv_sem=gather_sems.at[step - 1],
            device_id=(in_plane(step)[1], side), device_id_type=MESH,
        )
        copy.start()
        copies.append(copy)
    for copy in copies:
        copy.wait()
    swap = pltpu.make_async_remote_copy(
        src_ref=own_all, dst_ref=other_all, send_sem=pair_sems.at[0], recv_sem=pair_sems.at[1],
        device_id=(brick, 1 - side), device_id_type=MESH,
    )
    swap.start()
    swap.wait()

    mine = own_all[...].reshape(PLANE * rows, 128)
    theirs = other_all[...].reshape(PLANE * rows, 128)
    first, first_mixed = unpack(jnp.where(side == 0, mine, theirs))
    second, second_mixed = unpack(jnp.where(side == 0, theirs, mine))
    both = jnp.concatenate([first_mixed, second_mixed], axis=0)
    margin = jnp.concatenate(
        [jnp.concatenate([first, both], axis=1), jnp.concatenate([both.T, second], axis=1)], axis=0
    )
    scale = jnp.sqrt(jnp.sum(margin * margin, axis=(0, 1), keepdims=True) + epsilon)
    start = margin / scale
    value = three_less(0, start)
    inverse[...] = 0.5 * value
    put_left(left, value)
    put_right(right, start)
    current[...] = 0.5 * product_of(left, right, 2 * width)
    put_right(right, current[...])
    for step in range(1, NS_STEPS - 1):
        put_left(left, inverse[...])
        factor[...] = three_less(0, product_of(left, right, 2 * width))
        put_left(left, factor[...])
        current[...] = 0.5 * product_of(left, right, 2 * width)
        put_right(right, inverse[...])
        inverse[...] = 0.5 * product_of(left, right, 2 * width)
        put_right(right, current[...])
    first_row = pl.multiple_of(side * width, 16)
    put_left(left, inverse[pl.ds(first_row, width), :])
    factor[:width, :] = three_less(first_row, product_of(left, right, width))
    put_left(left, factor[:width, :])
    put_right(right, inverse[...])
    root_rows[...] = (0.5 * product_of(left, right, width)).astype(root_rows.dtype)
    for copy in rest:
        copy.wait()


def inverse_root(filtered):
    width, owned = filtered.shape
    f32 = jnp.float32
    rows = 384 // PLANE
    dma = pltpu.SemaphoreType.DMA
    return pl.pallas_call(
        root_kernel,
        name="inverse_root",
        out_shape=(
            jax.ShapeDtypeStruct((2 * width, owned), filtered.dtype),
            jax.ShapeDtypeStruct((width, 2 * width), jnp.bfloat16),
        ),
        in_specs=[block(VMEM)],
        out_specs=(block(VMEM),) * 2,
        scratch_shapes=[
            VMEM((384, 128), f32), VMEM((PLANE - 1, rows, 128), f32), VMEM((rows, 128), f32),
            VMEM((Z_SIZE, rows, 128), f32), VMEM((PLANE, rows, 128), f32), VMEM((PLANE, rows, 128), f32),
            VMEM((384, 128), f32), VMEM((384, 128), f32),
            VMEM((width, width), f32), VMEM((width, width), f32), VMEM((width, width), f32),
            VMEM((2 * width, 2 * width), f32), VMEM((2 * width, 2 * width), f32), VMEM((2 * width, 2 * width), f32),
            VMEM((2 * width, 12 * width), jnp.bfloat16), VMEM((12 * width, 2 * width), jnp.bfloat16),
            dma((2, 6)), dma((2,)), dma, dma((2 * PLANE + Z_SIZE - 3,)), dma((PLANE - 1,)), dma((Z_SIZE - 1,)),
            dma((PLANE - 1,)), dma((2,)),
        ],
        compiler_params=pltpu.CompilerParams(
            collective_id=0, has_side_effects=True, vmem_limit_bytes=32 << 20
        ),
    )(filtered)


def local(states, kinetic, potential, cell_nodes, face_map):
    filtered = filter_states(states, kinetic, potential, cell_nodes, face_map)
    every, root_rows = inverse_root(filtered)
    return jnp.dot(root_rows, every, preferred_element_type=jnp.float32)


def solution(mesh):
    in_specs = (P("state", "brick"), P(), P("brick"), P("brick", None), P("brick"))
    out_specs = P("state", "brick")
    return jax.shard_map(local, mesh=mesh, in_specs=in_specs, out_specs=out_specs, check_vma=False)
```

```python
import functools

import jax
import jax.numpy as jnp
from jax import lax
from jax.experimental import pallas as pl
from jax.experimental.pallas import tpu as pltpu
from jax.sharding import PartitionSpec as P

NS_STEPS = 3
LANES = 128
BATCH = 24
GROUP = 4
LIMIT = 20 << 20

cheb_center = 3.0
cheb_half = 7.0
epsilon = 1e-06

VMEM = pltpu.VMEM
SMEM = pltpu.SMEM


def block(space):
    return pl.BlockSpec(memory_space=space)


def passed_along(value, axis, steps):
    count = lax.axis_size(axis)
    pairs = [(source, (source + steps) % count) for source in range(count)]
    return lax.ppermute(value, axis, pairs)


def even(start):
    return pl.ds(start, LANES, stride=2)


def tile_start(tile):
    return pl.multiple_of(tile * (2 * LANES), 2 * LANES)


def padded(value):
    return jnp.concatenate([value, jnp.zeros((value.shape[0], LANES - value.shape[1]), value.dtype)], axis=1)


def packed_rows(faces):
    return faces * 3 // 2


def pack(out, tile, low, high):
    faces = out.shape[0] * 2 // 3
    lane = lax.broadcasted_iota(jnp.int32, (LANES // 2, LANES), 1)
    joined = jnp.where(lane < LANES // 2, high[: LANES // 2], pltpu.roll(high[LANES // 2 :], LANES // 2, axis=1))
    out[tile * LANES : (tile + 1) * LANES, :] = low.astype(out.dtype)
    out[faces + tile * LANES // 2 : faces + (tile + 1) * LANES // 2, :] = joined.astype(out.dtype)


def unpack_rows(ref, tile):
    faces = ref.shape[0] * 2 // 3
    low = ref[tile * LANES : (tile + 1) * LANES, :].astype(jnp.float32)
    joined = ref[faces + tile * LANES // 2 : faces + (tile + 1) * LANES // 2, :].astype(jnp.float32)
    return low, jnp.concatenate([joined, pltpu.roll(joined, LANES // 2, axis=1)], axis=0)


def pair_row(ref, row):
    return ref[pl.ds(row, 2), :]


def gather_rows(source, target, places):
    for row, place in enumerate(places):
        target[2 * row : 2 * row + 2, :] = pair_row(source, place())


def add_rows(total, addend, places):
    for first in range(0, len(places), BATCH):
        rows = range(first, min(first + BATCH, len(places)))
        at = [places[row]() for row in rows]
        sums = [pair_row(total, place) + addend[2 * row : 2 * row + 2, :] for place, row in zip(at, rows)]
        for place, value in zip(at, sums):
            total[pl.ds(place, 2), :] = value


def entries(index, count, *lead):
    start = lead[-1] if lead else 0
    return [functools.partial(lambda i: index[i], start + row) for row in range(count)]


def gather_faces(source, held, face, out):
    for tile in range(face.shape[0] // LANES):
        buffer = held.at[tile % 2]
        gather_rows(source, buffer, entries(face, LANES, tile * LANES))
        pack(out, tile, buffer[even(0), :], buffer[even(1), :])


def fill_table(width, states, table):
    def one(tile, carry):
        nodes = pl.ds(pl.multiple_of(tile * LANES, LANES), LANES)
        low = states[:LANES, nodes].astype(jnp.float32)
        high = states[LANES:width, nodes].astype(jnp.float32)
        high = jnp.concatenate([high, jnp.zeros((2 * LANES - width, LANES), jnp.float32)], axis=0)
        start = tile_start(tile)
        table[even(start), :] = low.T
        table[even(start + 1), :] = high.T
        return carry

    lax.fori_loop(0, states.shape[1] // LANES, one, 0, unroll=2)


def spread_kernel(potential, factor):
    def one(tile, carry):
        value = jnp.broadcast_to(potential[pl.ds(tile, 1), :], (LANES, LANES)).T - cheb_center
        start = tile_start(tile)
        factor[even(start), :] = value
        factor[even(start + 1), :] = value
        return carry

    lax.fori_loop(0, potential.shape[0], one, 0, unroll=2)


def copy_rows(source, target, count):
    def take(tile, carry):
        rows = pl.ds(tile_start(tile), 2 * LANES)
        target[rows, :] = source[rows, :]
        return carry

    lax.fori_loop(0, count // (2 * LANES), take, 0)


def faces_kernel(width, states, face, faces, table, held):
    fill_table(width, states, table)
    gather_faces(table, held, face, faces)


def start_sums(table, total, factor, owned, ghosts):
    def one(tile, carry):
        rows = pl.ds(pl.multiple_of(tile * LANES, LANES), LANES)
        total[rows, :] = factor[rows, :] * table[rows, :]
        return carry

    lax.fori_loop(0, 2 * owned // LANES, one, 0, unroll=2)
    total[2 * owned :, :] = jnp.zeros((2 * ghosts, LANES), jnp.float32)


def apply_cells(table, total, kinetic, index, slots, held, product, places, sems):
    depth = kinetic.shape[0]
    groups, cells, _ = index.shape
    for side in range(2):
        held[side, 2 * slots :, :] = jnp.zeros((2 * (depth - slots), LANES), jnp.float32)

    def fetch(group, side):
        return pltpu.make_async_copy(index.at[group], places.at[side], sems.at[side])

    def one_group(group, side):
        fetch(group, side).wait()
        fetch(jnp.minimum(group + 1, groups - 1), 1 - side).start()
        for cell in range(cells):
            at = [functools.partial(lambda i: places[side, cell, i], row) for row in range(slots)]
            values, result = held.at[cell % 2], product.at[cell % 2]
            gather_rows(table, values, at)
            operand = jnp.concatenate(
                [values[pl.ds(0, depth, stride=2), :], values[pl.ds(1, depth, stride=2), :]], axis=1
            ).astype(jnp.bfloat16)
            answer = jnp.dot(kinetic[...], operand, preferred_element_type=jnp.float32)
            result[pl.ds(0, depth, stride=2), :] = answer[:, :LANES]
            result[pl.ds(1, depth, stride=2), :] = answer[:, LANES:]
            add_rows(total, result, at)

    fetch(0, 0).start()

    def two_groups(step, carry):
        one_group(2 * step, 0)
        one_group(2 * step + 1, 1)
        return carry

    lax.fori_loop(0, groups // 2, two_groups, 0)
    fetch(groups - 1, groups % 2).wait()


def give_ghosts(total, owned, out):
    for tile in range(out.shape[0] * 2 // 3 // LANES):
        start = 2 * owned + tile * 2 * LANES
        pack(out, tile, total[even(start), :], total[even(start + 1), :])


def first_kernel(
    width, slots, states, ghosts, potential, kinetic, index, face, sums, ghost_out, face_out,
    table, total, held, product, places, sems,
):
    owned = states.shape[1]
    face_count = face.shape[0]
    fill_table(width, states, table)
    for tile in range(face_count // LANES):
        start = 2 * owned + tile * 2 * LANES
        low, high = unpack_rows(ghosts, tile)
        table[even(start), :] = low
        table[even(start + 1), :] = high
    start_sums(table, total, potential, owned, face_count)
    apply_cells(table, total, kinetic, index, slots, held, product, places, sems)
    give_ghosts(total, owned, ghost_out)
    gather_faces(total, held, face, face_out)
    copy_rows(total, sums, total.shape[0])


def add_returned(total, returned, face, held):
    for tile in range(face.shape[0] // LANES):
        low, high = unpack_rows(returned, tile)
        buffer = held.at[tile % 2]
        buffer[even(0), :] = low
        buffer[even(1), :] = high
        add_rows(total, buffer, entries(face, LANES, tile * LANES))


def second_kernel(
    owned, slots, given, returned, ghost_sums, potential, kinetic, index, face, summed, sums, ghost_out,
    table, total, held, product, places, sems,
):
    face_count = face.shape[0]
    rows_all = table.shape[0]
    add_returned(summed, returned, face, held)
    for tile in range(face_count // LANES):
        start = 2 * owned + tile * 2 * LANES
        low, high = unpack_rows(ghost_sums, tile)
        summed[even(start), :] = summed[even(start), :] + low
        summed[even(start + 1), :] = summed[even(start + 1), :] + high

    def scale(tile, carry):
        rows = pl.ds(tile_start(tile), 2 * LANES)
        table[rows, :] = (summed[rows, :] / cheb_half).astype(jnp.bfloat16).astype(jnp.float32)
        return carry

    lax.fori_loop(0, rows_all // (2 * LANES), scale, 0)
    start_sums(table, total, potential, owned, face_count)
    apply_cells(table, total, kinetic, index, slots, held, product, places, sems)
    give_ghosts(total, owned, ghost_out)
    copy_rows(total, sums, 2 * owned)


def last_kernel(width, given, states, returned, face, filtered, total, held):
    owned = filtered.shape[1]
    add_returned(total, returned, face, held)

    def one(tile, carry):
        start = tile_start(tile)
        nodes = pl.ds(pl.multiple_of(tile * LANES, LANES), LANES)
        low = (2.0 * total[even(start), :] / cheb_half).T
        high = (2.0 * total[even(start + 1), :] / cheb_half).T[: width - LANES, :]
        filtered[:LANES, nodes] = (low - states[:LANES, nodes].astype(jnp.float32)).astype(filtered.dtype)
        filtered[LANES:width, nodes] = (high - states[LANES:width, nodes].astype(jnp.float32)).astype(filtered.dtype)
        return carry

    lax.fori_loop(0, owned // LANES, one, 0, unroll=2)


def filter_states(states, kinetic, potential, cell_nodes, face_map):
    width, owned = states.shape
    cells, slots = cell_nodes.shape
    face_count = face_map.shape[0]
    depth = -(-slots // 16) * 16
    f32 = jnp.float32
    face = 2 * face_map
    index = jnp.pad(2 * cell_nodes, ((0, 0), (0, 384 - slots))).reshape(-1, GROUP, 384)
    potential = pl.pallas_call(
        spread_kernel,
        name="spread_potential",
        out_shape=jax.ShapeDtypeStruct((2 * owned, LANES), f32),
        in_specs=[block(VMEM)],
        out_specs=block(VMEM),
        compiler_params=pltpu.CompilerParams(vmem_limit_bytes=LIMIT),
        cost_estimate=pl.CostEstimate(flops=2 * owned * LANES, bytes_accessed=24 * owned * LANES, transcendentals=0),
    )(potential.reshape(-1, LANES))
    kinetic = jnp.pad(kinetic, ((0, depth - slots), (0, depth - slots)))
    rows_all = 2 * (owned + face_count)
    field = jax.ShapeDtypeStruct((rows_all, LANES), f32)
    sums = jax.ShapeDtypeStruct((packed_rows(face_count), LANES), f32)
    table = VMEM((rows_all, LANES), f32)
    faces_held = VMEM((2, 2 * LANES, LANES), f32)
    work = [
        VMEM((2, 2 * depth, LANES), f32), VMEM((2, 2 * depth, LANES), f32),
        SMEM((2, GROUP, 384), jnp.int32), pltpu.SemaphoreType.DMA((2,)),
    ]
    params = pltpu.CompilerParams(vmem_limit_bytes=LIMIT)

    faces = pl.pallas_call(
        functools.partial(faces_kernel, width),
        name="gather_faces",
        out_shape=jax.ShapeDtypeStruct(sums.shape, states.dtype),
        in_specs=[block(VMEM), block(SMEM)],
        out_specs=block(VMEM),
        scratch_shapes=[VMEM((2 * owned, LANES), f32), faces_held],
        compiler_params=params,
    )(states, face)
    ghosts = passed_along(faces, "brick", -1)
    first, ghost_part, face_part = pl.pallas_call(
        functools.partial(first_kernel, width, slots),
        name="first_apply",
        out_shape=(field, sums, sums),
        in_specs=[block(VMEM)] * 4 + [block(pl.ANY), block(SMEM)],
        out_specs=(block(VMEM),) * 3,
        scratch_shapes=[table, table] + work,
        compiler_params=params,
    )(states, ghosts, potential, kinetic, index, face)
    returned = passed_along(ghost_part, "brick", 1)
    ghost_sums = passed_along(face_part, "brick", -1)
    _, second, ghost_part = pl.pallas_call(
        functools.partial(second_kernel, owned, slots),
        name="second_apply",
        out_shape=(field, jax.ShapeDtypeStruct((2 * owned, LANES), f32), sums),
        in_specs=[block(VMEM)] * 5 + [block(pl.ANY), block(SMEM)],
        out_specs=(block(VMEM),) * 3,
        input_output_aliases={0: 0},
        scratch_shapes=[table, table] + work,
        compiler_params=params,
    )(first, returned, ghost_sums, potential, kinetic, index, face)
    returned = passed_along(ghost_part, "brick", 1)
    return pl.pallas_call(
        functools.partial(last_kernel, width),
        name="finish_filter",
        out_shape=(
            jax.ShapeDtypeStruct((width, owned), jnp.bfloat16),
            jax.ShapeDtypeStruct((2 * owned, LANES), f32),
        ),
        in_specs=[block(VMEM)] * 3 + [block(SMEM)],
        out_specs=(block(VMEM),) * 2,
        input_output_aliases={0: 1},
        scratch_shapes=[faces_held],
        compiler_params=params,
    )(second, states, returned, face)[0]


X_SIZE, Y_SIZE, Z_SIZE = 4, 4, 8
PLANE = X_SIZE * Y_SIZE
MESH = pl.DeviceIdType.MESH
EXACT = lax.Precision.HIGHEST
CHUNK = 768


def across(left, right):
    return lax.dot_general(left, right, (((1,), (1,)), ((), ())), preferred_element_type=jnp.float32)


def product_of(left, right):
    return jnp.dot(left, right, precision=EXACT, preferred_element_type=jnp.float32)


def unpack(packed):
    corner = packed[128:192, :]
    right = jnp.concatenate([corner.T, packed[288:352, 64:128]], axis=0)
    square = jnp.concatenate([packed[:192, :], right], axis=1)
    mixed = jnp.concatenate([packed[192:288, :], packed[288:384, :64]], axis=1)
    return square, mixed


def root_kernel(
    own, every, root_rows,
    share, inbox, part, levels, own_all, other_all, square, mixed, current, inverse,
    state_sems, here_sem, send_sems, plane_sems, level_sems, gather_sems, pair_sems,
):
    brick, side = lax.axis_index("brick"), lax.axis_index("state")
    width, owned = own.shape
    half = width // 2
    y, z, x = brick % Y_SIZE, (brick // Y_SIZE) % Z_SIZE, brick // (Y_SIZE * Z_SIZE)
    place = x * Y_SIZE + y

    def in_plane(step):
        target = (place + step) % PLANE
        return target, ((target // Y_SIZE) * Z_SIZE + z) * Y_SIZE + target % Y_SIZE

    def in_line(step):
        return (x * Z_SIZE + (z + step) % Z_SIZE) * Y_SIZE + y

    barrier = pltpu.get_barrier_semaphore()
    pl.semaphore_signal(barrier, inc=1, device_id=(brick, 1 - side), device_id_type=MESH)
    for step in range(1, PLANE):
        pl.semaphore_signal(barrier, inc=1, device_id=(in_plane(step)[1], side), device_id_type=MESH)
    for step in range(1, Z_SIZE):
        pl.semaphore_signal(barrier, inc=1, device_id=(in_line(step), side), device_id_type=MESH)
    pl.semaphore_wait(barrier, PLANE + Z_SIZE - 1)

    pieces = 3
    piece = owned // pieces
    place_here = pl.ds(pl.multiple_of(side * width, 16), width)
    here = pltpu.make_async_copy(own, every.at[place_here, :], here_sem)
    here.start()
    states = []
    for number in range(pieces):
        columns = pl.ds(number * piece, piece)
        copy = pltpu.make_async_remote_copy(
            src_ref=own.at[:, columns], dst_ref=every.at[place_here, columns],
            send_sem=state_sems.at[0, number], recv_sem=state_sems.at[1, number],
            device_id=(brick, 1 - side), device_id_type=MESH,
        )
        copy.start()
        states.append(copy)

    square[...] = jnp.zeros_like(square)
    mixed[...] = jnp.zeros_like(mixed)

    def add_square(number, carry):
        values = own[:, pl.ds(pl.multiple_of(number * CHUNK, CHUNK), CHUNK)]
        square[...] += across(values, values)
        return carry

    lax.fori_loop(0, owned // CHUNK, add_square, 0)
    here.wait()
    some = pl.ds(pl.multiple_of(side * half, 16), half)
    for number, copy in enumerate(states):
        copy.wait()

        def add_mixed(step, carry):
            columns = pl.ds(pl.multiple_of(number * piece + step * CHUNK, CHUNK), CHUNK)
            mixed[...] += across(every[some, columns], every[width:, columns])
            return carry

        lax.fori_loop(0, piece // CHUNK, add_mixed, 0)

    share[:192, :] = square[:, :128]
    share[192:288, :] = mixed[:, :128]
    share[288:352, :] = jnp.concatenate([mixed[:64, 128:], square[128:, 128:]], axis=1)
    share[352:384, :] = jnp.concatenate([mixed[64:, 128:], jnp.zeros((32, 64), jnp.float32)], axis=1)

    rows = share.shape[0] // PLANE
    copies = []
    for step in range(1, PLANE):
        target, chip = in_plane(step)
        copy = pltpu.make_async_remote_copy(
            src_ref=share.at[pl.ds(pl.multiple_of(target * rows, 8), rows), :], dst_ref=inbox.at[step - 1],
            send_sem=send_sems.at[step - 1], recv_sem=plane_sems.at[step - 1],
            device_id=(chip, side), device_id_type=MESH,
        )
        copy.start()
        copies.append(copy)
    value = share[pl.ds(pl.multiple_of(place * rows, 8), rows), :]
    for copy in copies:
        copy.wait()
    for step in range(PLANE - 1):
        value = value + inbox[step]
    part[...] = value
    levels[z] = value
    copies = []
    for step in range(1, Z_SIZE):
        copy = pltpu.make_async_remote_copy(
            src_ref=part, dst_ref=levels.at[z],
            send_sem=send_sems.at[PLANE - 2 + step], recv_sem=level_sems.at[step - 1],
            device_id=(in_line(step), side), device_id_type=MESH,
        )
        copy.start()
        copies.append(copy)
    for copy in copies:
        copy.wait()
    value = levels[0]
    for step in range(1, Z_SIZE):
        value = value + levels[step]
    own_all[place] = value
    copies = []
    for step in range(1, PLANE):
        copy = pltpu.make_async_remote_copy(
            src_ref=own_all.at[place], dst_ref=own_all.at[place],
            send_sem=send_sems.at[PLANE + Z_SIZE - 3 + step], recv_sem=gather_sems.at[step - 1],
            device_id=(in_plane(step)[1], side), device_id_type=MESH,
        )
        copy.start()
        copies.append(copy)
    for copy in copies:
        copy.wait()
    swap = pltpu.make_async_remote_copy(
        src_ref=own_all, dst_ref=other_all, send_sem=pair_sems.at[0], recv_sem=pair_sems.at[1],
        device_id=(brick, 1 - side), device_id_type=MESH,
    )
    swap.start()
    swap.wait()

    mine = own_all[...].reshape(PLANE * rows, 128)
    theirs = other_all[...].reshape(PLANE * rows, 128)
    first, first_mixed = unpack(jnp.where(side == 0, mine, theirs))
    second, second_mixed = unpack(jnp.where(side == 0, theirs, mine))
    both = jnp.concatenate([first_mixed, second_mixed], axis=0)
    margin = jnp.concatenate(
        [jnp.concatenate([first, both], axis=1), jnp.concatenate([both.T, second], axis=1)], axis=0
    )
    scale = jnp.sqrt(jnp.sum(margin * margin, axis=(0, 1), keepdims=True) + epsilon)
    total = margin.shape[0]
    row_ids = lax.broadcasted_iota(jnp.int32, (total, total), 0)
    column_ids = lax.broadcasted_iota(jnp.int32, (total, total), 1)
    three = jnp.where(row_ids == column_ids, 3.0, 0.0)
    start = margin / scale
    factor = three - start
    current[...] = 0.5 * product_of(factor, start)
    inverse[...] = 0.5 * factor
    for step in range(1, NS_STEPS - 1):
        factor = three - product_of(inverse[...], current[...])
        current[...] = 0.5 * product_of(factor, current[...])
        inverse[...] = 0.5 * product_of(factor, inverse[...])
    mine = pl.ds(pl.multiple_of(side * width, 8), width)
    row_ids = lax.broadcasted_iota(jnp.int32, (width, total), 0) + side * width
    column_ids = lax.broadcasted_iota(jnp.int32, (width, total), 1)
    factor = jnp.where(row_ids == column_ids, 3.0, 0.0) - product_of(inverse[mine, :], current[...])
    root_rows[...] = (0.5 * product_of(factor, inverse[...])).astype(root_rows.dtype)


def inverse_root(filtered):
    width, owned = filtered.shape
    f32 = jnp.float32
    rows = 384 // PLANE
    dma = pltpu.SemaphoreType.DMA
    return pl.pallas_call(
        root_kernel,
        name="inverse_root",
        out_shape=(
            jax.ShapeDtypeStruct((2 * width, owned), filtered.dtype),
            jax.ShapeDtypeStruct((width, 2 * width), jnp.bfloat16),
        ),
        in_specs=[block(VMEM)],
        out_specs=(block(VMEM),) * 2,
        scratch_shapes=[
            VMEM((384, 128), f32), VMEM((PLANE - 1, rows, 128), f32), VMEM((rows, 128), f32),
            VMEM((Z_SIZE, rows, 128), f32), VMEM((PLANE, rows, 128), f32), VMEM((PLANE, rows, 128), f32),
            VMEM((width, width), f32), VMEM((width // 2, width), f32),
            VMEM((2 * width, 2 * width), f32), VMEM((2 * width, 2 * width), f32),
            dma((2, 3)), dma, dma((2 * PLANE + Z_SIZE - 3,)), dma((PLANE - 1,)), dma((Z_SIZE - 1,)),
            dma((PLANE - 1,)), dma((2,)),
        ],
        compiler_params=pltpu.CompilerParams(
            collective_id=0, has_side_effects=True, vmem_limit_bytes=32 << 20
        ),
    )(filtered)


def local(states, kinetic, potential, cell_nodes, face_map):
    filtered = filter_states(states, kinetic, potential, cell_nodes, face_map)
    every, root_rows = inverse_root(filtered)
    return jnp.dot(root_rows, every, preferred_element_type=jnp.float32)


def solution(mesh):
    in_specs = (P("state", "brick"), P(), P("brick"), P("brick", None), P("brick"))
    out_specs = P("state", "brick")
    return jax.shard_map(local, mesh=mesh, in_specs=in_specs, out_specs=out_specs, check_vma=False)
```
